128 devices in a mesh: section: 32 (over y, x, z_lo), tensor: 4 (over z_hi, core).
Axes of the slice: x: 4, y: 4, z: 4 (z_hi: 2, z_lo: 2; z = z_hi * 2 + z_lo), core: 2. Of those that a mesh axis runs over, the one named last changes fastest.
Arguments:
- weights: bfloat16 [32, 4096, 4096], P('section', 'tensor'), may hold values from -0.09375 to 0.09375
- filters: float32 [32, 32, 128], P('section'), may hold values from -0.5 to 0.5
- down_input: bfloat16 [32, 512, 4096], P('section', 'tensor'), may hold values from -6 to 6
- down_cot: bfloat16 [32, 512, 4096], P('section', 'tensor'), may hold values from -6 to 6
- up_input: bfloat16 [32, 512, 4096], P('section', 'tensor'), may hold values from -6 to 6
- up_cot: bfloat16 [32, 512, 4096], P('section', 'tensor'), may hold values from -6 to 6
Outputs:
- weight_grad: bfloat16 [32, 4096, 4096], P('section', 'tensor')
- filter_grad: float32 [32, 32, 128], P('section')
- down_passed: bfloat16 [32, 512, 4096], P('section', 'tensor')
- up_passed: bfloat16 [32, 512, 4096], P('section', 'tensor')
The draws below stay inside these ranges and needn't reach their ends.
All inputs are finite; a program needn't handle non-finite values.
Results may differ from the reference program's by a relative error of at most 0.014.
Values may be sent and summed in bfloat16 or wider, within the bound.
A program may use at most 192 MiB of HBM per device.

```python
import jax
import jax.numpy as jnp
from jax import lax

D = 4096
K = 128
GROUPS = 32
TOKENS = 512
LAYERS = 32


def levels(stream_key, extent, shards, least, high):
    gain, own = 1.0, jax.random.fold_in(stream_key, 6)
    for position, blocks in shards:
        steps = jnp.exp(jax.random.uniform(jax.random.fold_in(own, position), (blocks,), jnp.float32, least / len(shards), high / len(shards)))
        gain = gain * jnp.repeat(steps, extent[position] // blocks).reshape([-1 if axis == position else 1 for axis in range(len(extent))])
    return gain


def noise(key, extent, deviation, reach, split=(), held_as=jnp.bfloat16):
    gain = levels(key, extent, split, -0.22, 0.18) if split else 1.0
    result = jax.random.normal(key, extent, jnp.float32) * deviation * gain
    return jnp.minimum(jnp.maximum(result, -reach), reach).astype(held_as)


def setup_inputs(seed: int = 0) -> dict:
    key_of = jax.random.split(jax.random.key(seed), 7)
    weights = noise(key_of[0], (LAYERS, D, D), D ** -0.5, 0.09375, ((0, 32), (1, 4)))
    filters = noise(key_of[1], (LAYERS, GROUPS, K), K ** -0.5, 0.5, ((0, 32),), jnp.float32)
    down_input = noise(key_of[2], (LAYERS, TOKENS, D), 1.0, 6.0, ((0, 32), (1, 4)))
    down_cot = noise(key_of[3], (LAYERS, TOKENS, D), 1.0, 6.0, ((0, 32), (1, 4)))
    up_input = noise(key_of[4], (LAYERS, TOKENS, D), 1.0, 6.0, ((0, 32), (1, 4)))
    up_cot = noise(key_of[5], (LAYERS, TOKENS, D), 1.0, 6.0, ((0, 32), (1, 4)))
    return {"weights": weights, "filters": filters, "down_input": down_input, "down_cot": down_cot, "up_input": up_input, "up_cot": up_cot}


epsilon = 1e-06

def causal_mix(extended, kernel, count):
    taps_total = kernel.shape[0]

    def add_tap(tap_index, running):
        window = lax.dynamic_slice_in_dim(extended, taps_total - 1 - tap_index, count, 0)
        return running + lax.dynamic_index_in_dim(kernel, tap_index, 0, keepdims=False) * window
    return lax.fori_loop(0, taps_total, add_tap, jnp.zeros((count,) + extended.shape[1:], jnp.float32))

def ahead_mix(extended, kernel, count):
    taps_total = kernel.shape[0]

    def add_tap(tap_index, running):
        window = lax.dynamic_slice_in_dim(extended, tap_index, count, 0)
        return running + lax.dynamic_index_in_dim(kernel, tap_index, 0, keepdims=False) * window
    return lax.fori_loop(0, taps_total, add_tap, jnp.zeros((count,) + extended.shape[1:], jnp.float32))

def layer_grads(inputs, cotangent, weight, filter_taps):
    count = inputs.shape[0]
    model_width = inputs.shape[1]
    group_count = filter_taps.shape[0]
    taps_total = filter_taps.shape[1]
    input_wide = inputs.astype(jnp.float32)
    inverse_rms = lax.rsqrt(lax.optimization_barrier(jnp.mean(input_wide * input_wide, axis=1, keepdims=True)) + epsilon)
    normed = input_wide * inverse_rms
    normed_b = normed.astype(jnp.bfloat16)
    values = jnp.dot(normed_b, weight, preferred_element_type=jnp.float32)
    kernel = jnp.repeat(jnp.transpose(filter_taps), model_width // group_count, axis=1)
    extended = jnp.concatenate([jnp.zeros((taps_total - 1, model_width), jnp.float32), values], axis=0)
    convolved = causal_mix(extended, kernel, count)
    cot_wide = cotangent.astype(jnp.float32)
    grad_mix = cot_wide * normed
    grad_ext = jnp.concatenate([grad_mix, jnp.zeros((taps_total - 1, model_width), jnp.float32)], axis=0)
    grad_values = ahead_mix(grad_ext, kernel, count)

    def one_tap(tap_index):
        window = lax.dynamic_slice_in_dim(extended, taps_total - 1 - tap_index, count, 0)
        return lax.optimization_barrier(jnp.sum(grad_mix * window, axis=0))
    per_tap = lax.map(one_tap, jnp.arange(taps_total, dtype=jnp.int32))
    tap_grad = jnp.transpose(lax.optimization_barrier(jnp.sum(per_tap.reshape(taps_total, group_count, -1), axis=2)))
    grad_values_b = grad_values.astype(jnp.bfloat16)
    weight_part = jnp.dot(jnp.transpose(normed_b), grad_values_b, preferred_element_type=jnp.float32)
    grad_total = cot_wide * convolved + jnp.dot(grad_values_b, jnp.transpose(weight), preferred_element_type=jnp.float32)
    projection_mean = lax.optimization_barrier(jnp.mean(grad_total * normed, axis=1, keepdims=True))
    grad_in = (cot_wide + inverse_rms * (grad_total - normed * projection_mean)).astype(jnp.bfloat16)
    return (grad_in, weight_part, tap_grad)

def reference(weights, filters, down_input, down_cot, up_input, up_cot):

    def per_layer(operands):
        weight, filter_taps, down_in, down_ct, up_in, up_ct = operands
        down_grad, down_weight, down_taps = layer_grads(down_in, down_ct, weight, filter_taps)
        up_grad, up_weight, up_taps = layer_grads(up_in, up_ct, weight, filter_taps)
        return (down_grad, up_grad, (down_weight + up_weight).astype(jnp.bfloat16), down_taps + up_taps)
    down_grads, up_grads, weight_grad, filter_grad = lax.map(per_layer, (weights, filters, down_input, down_cot, jnp.flip(up_input, 0), jnp.flip(up_cot, 0)))
    zero_block = jnp.zeros((1,) + down_grads.shape[1:], jnp.bfloat16)
    down_passed = jnp.concatenate([down_grads[1:], zero_block], axis=0)
    up_passed = jnp.concatenate([zero_block, jnp.flip(up_grads[1:], 0)], axis=0)
    return (weight_grad, filter_grad, down_passed, up_passed)
```

```python
import functools

import jax
import jax.numpy as jnp
from jax import lax
from jax.experimental import pallas as pl
from jax.experimental.pallas import tpu as pltpu
from jax.sharding import PartitionSpec as P

epsilon = 1e-06
MESH = pl.DeviceIdType.MESH
bf16 = jnp.bfloat16
f32 = jnp.float32
NT = 4


def contract_last(a, b):
    return lax.dot_general(a, b, (((1,), (1,)), ((), ())), preferred_element_type=f32)


def matmul(a, b):
    return jnp.dot(a, b, preferred_element_type=f32)


def kernel(
    sections,
    w_hbm, f_ref, xd_hbm, cd_hbm, xu_hbm, cu_hbm,
    dw_hbm, fg_hbm, od_hbm, ou_hbm,
    W, X, C, R, OWN, U, RS, T, TC, NBT, GV, VS, V, VR, G, PM, OS, FG, DW,
    g_send, g_recv, r_send, r_recv, u_send, u_recv, v_send, v_recv,
    gv_send, gv_recv, pm_send, pm_recv, o_send, o_recv, fg_send, fg_recv,
    w_sem, own_sem, dw_sem,
):
    S = sections
    s = lax.axis_index("section")
    t = lax.axis_index("tensor")
    h = t // 2
    c = t % 2
    sib = (s, h * 2 + (1 - c))
    TB, D = xd_hbm.shape
    BW = D // NT
    CW = 2 * BW
    TOK = NT * TB
    groups = f_ref.shape[0]
    per_block = groups // NT
    n_groups = 2 * per_block
    gw = D // groups
    flip = s + 1 - 2 * (s % 2)
    mirror = S - 1 - s
    relay = mirror + 1 - 2 * (mirror % 2)
    prev_s = lax.rem(s + S - 1, S)
    next_s = lax.rem(s + 1, S)
    up_s = lax.rem(S - s, S)
    up_self = up_s == s

    barrier = pltpu.get_barrier_semaphore()

    def greet(dev):
        pl.semaphore_signal(barrier, inc=1, device_id=dev, device_id_type=MESH)

    for q in range(1, NT):
        greet((s, lax.rem(t + q, NT)))
    greet((relay, t))
    for q in range(NT):
        greet((flip, q))
        greet((next_s, q))
    for q in range(NT):
        own = jnp.logical_and(up_self, t == q)

        @pl.when(jnp.logical_not(own))
        def _():
            greet((up_s, q))

    w_copy = pltpu.make_async_copy(w_hbm, W, w_sem)
    w_copy.start()
    own_copy = pltpu.make_async_copy(xd_hbm, OWN, own_sem)
    own_copy.start()
    pl.semaphore_wait(barrier, jnp.where(up_self, 15, 16))

    my_rows = pl.ds(pl.multiple_of(t * TB, TB), TB)

    def piece(src, dst_ref, mb, arr, q, i, dev, src_t):
        return pltpu.make_async_remote_copy(
            src_ref=src.at[:, pl.ds((2 * i + q % 2) * BW, BW)],
            dst_ref=dst_ref.at[mb, pl.ds(pl.multiple_of(src_t * TB, TB), TB), pl.ds(i * BW, BW)],
            send_sem=g_send.at[mb, arr, q, i],
            recv_sem=g_recv.at[mb, arr, src_t, i],
            device_id=dev,
            device_id_type=MESH,
        )

    def local_piece(src, dst_ref, mb, arr, q, i):
        return pltpu.make_async_copy(
            src.at[:, pl.ds((2 * i + q % 2) * BW, BW)],
            dst_ref.at[mb, pl.ds(q * TB, TB), pl.ds(i * BW, BW)],
            g_recv.at[mb, arr, q, i],
        )

    for arr, (src, dst) in enumerate(((xd_hbm, X), (cd_hbm, C))):
        for q in range(NT):
            @pl.when(t != q)
            def _():
                for i in range(2):
                    piece(src, dst, 0, arr, q, i, (s, q), t).start()

            @pl.when(t == q)
            def _():
                for i in range(2):
                    local_piece(src, dst, 0, arr, q, i).start()

    def relay_copy(arr):
        return pltpu.make_async_remote_copy(
            src_ref=(xu_hbm, cu_hbm)[arr], dst_ref=U.at[arr],
            send_sem=u_send.at[arr], recv_sem=u_recv.at[arr],
            device_id=(relay, t), device_id_type=MESH,
        )

    for arr in range(2):
        relay_copy(arr).start()

    def inverse_rms(ref):
        def step(j, acc):
            x = ref[:, pl.ds(pl.multiple_of(j * gw, gw), gw)].astype(f32)
            return acc + x * x
        acc = lax.fori_loop(0, D // gw, step, jnp.zeros((TB, gw), f32))
        mean = jnp.sum(acc, axis=1, keepdims=True) / D
        return jnp.broadcast_to(lax.rsqrt(mean + epsilon), (TB, 128))

    def r_copy(mb, q, dev):
        return pltpu.make_async_remote_copy(
            src_ref=RS.at[mb], dst_ref=R.at[mb, my_rows, :],
            send_sem=r_send.at[mb, q], recv_sem=r_recv.at[mb, t],
            device_id=dev, device_id_type=MESH,
        )

    own_copy.wait()
    RS[0] = inverse_rms(OWN)
    for q in range(NT):
        @pl.when(t != q)
        def _():
            r_copy(0, q, (s, q)).start()

        @pl.when(t == q)
        def _():
            R[0, q * TB : (q + 1) * TB, :] = RS[0]

    rows = lax.broadcasted_iota(jnp.int32, (TB, 2 * TB), 0)

    def build(gi, carry):
        g = (gi // per_block * 2 + c) * per_block + lax.rem(gi, per_block)
        taps = jnp.broadcast_to(f_ref[pl.ds(g, 1), :], (TB, TB))
        x = jnp.concatenate([taps, jnp.zeros((TB, TB), f32)], axis=1)
        step = 1
        while step < TB:
            x = jnp.where((rows & step) != 0, pltpu.roll(x, step, 1), x)
            step *= 2
        T[gi] = x.astype(bf16)
        TC[gi] = jnp.concatenate([x[:, TB:].T, x[:, :TB].T], axis=1).astype(bf16)
        return carry

    lax.fori_loop(0, n_groups, build, 0)
    FG[...] = jnp.zeros_like(FG)

    def gather_wait(mb):
        for arr, dst in enumerate((X, C)):
            for q in range(NT):
                for i in range(2):
                    pltpu.make_async_copy(
                        dst.at[mb, pl.ds(q * TB, TB), pl.ds(i * BW, BW)],
                        dst.at[mb, pl.ds(q * TB, TB), pl.ds(i * BW, BW)],
                        g_recv.at[mb, arr, q, i],
                    ).wait()
        for q in range(NT):
            def wait_r():
                pltpu.make_async_copy(RS.at[mb], R.at[mb, pl.ds(q * TB, TB), :], r_recv.at[mb, q]).wait()
            if mb == 0:
                pl.when(t != q)(wait_r)
            else:
                wait_r()

    gather_wait(0)

    for arr in range(2):
        relay_copy(arr).wait_recv()
        for q in range(NT):
            for i in range(2):
                piece(U.at[arr], (X, C)[arr], 1, arr, q, i, (flip, q), t).start()
    RS[1] = inverse_rms(U.at[0])
    for q in range(NT):
        r_copy(1, q, (flip, q)).start()

    def cols(j, width=gw):
        return pl.ds(pl.multiple_of(j * width, width), width)

    def natural(gi):
        return (gi // per_block * 2 + c) * per_block + lax.rem(gi, per_block)

    def windows(x):
        return jnp.concatenate([x[i * TB : (i + 2) * TB] for i in range(NT)], axis=1)

    zero_block = jnp.zeros((TB, gw), bf16)

    def gv_copy(mb, i):
        blk = pl.ds(pl.multiple_of((2 * i + c) * BW, BW), BW)
        return pltpu.make_async_remote_copy(
            src_ref=GV.at[pl.ds(mb * TOK, TOK), blk], dst_ref=GV.at[pl.ds(mb * TOK, TOK), blk],
            send_sem=gv_send.at[mb, i], recv_sem=gv_recv.at[mb, i],
            device_id=sib, device_id_type=MESH,
        )

    def v_copy(mb):
        return pltpu.make_async_remote_copy(
            src_ref=VS, dst_ref=VR.at[mb],
            send_sem=v_send.at[mb], recv_sem=v_recv.at[mb],
            device_id=sib, device_id_type=MESH,
        )

    def pm_copy(mb):
        return pltpu.make_async_remote_copy(
            src_ref=PM.at[mb, 0], dst_ref=PM.at[mb, 1],
            send_sem=pm_send.at[mb], recv_sem=pm_recv.at[mb],
            device_id=sib, device_id_type=MESH,
        )

    VN = min(512, BW)
    RN = min(256, BW)

    def layer(mb):
        def prep(gi, carry):
            n = X[mb, :, cols(gi)].astype(f32) * R[mb]
            gm = (C[mb, :, cols(gi)].astype(f32) * n).astype(bf16)
            X[mb, :, cols(gi)] = n.astype(bf16)
            w = windows(jnp.concatenate([gm, zero_block], axis=0))
            gv = matmul(T[gi], w).astype(bf16)
            for i in range(NT):
                GV[mb * TOK + i * TB : mb * TOK + (i + 1) * TB, cols(natural(gi))] = gv[:, i * gw : (i + 1) * gw]
            return carry

        lax.fori_loop(0, n_groups, prep, 0)
        for i in range(2):
            gv_copy(mb, i).start()

        own_cols = pl.ds(pl.multiple_of(h * BW, BW), BW)

        def sib_values(j, carry):
            src = (j // (BW // VN) * 2 + (1 - c)) * (BW // VN) + lax.rem(j, BW // VN)
            VS[:, cols(j, VN)] = matmul(X[mb, :, own_cols], W[:, cols(src, VN)]).astype(bf16)
            return carry

        def own_values(j, carry):
            src = (j // (BW // VN) * 2 + c) * (BW // VN) + lax.rem(j, BW // VN)
            V[:, cols(j, VN)] = matmul(X[mb, :, own_cols], W[:, cols(src, VN)]).astype(bf16)
            return carry

        lax.fori_loop(0, CW // VN, sib_values, 0)
        v_copy(mb).start()
        lax.fori_loop(0, CW // VN, own_values, 0)

        def turn(j, carry):
            n = X[mb, :, cols(h * per_block + j)].astype(f32)
            NBT[cols(j), mb * TOK : (mb + 1) * TOK] = n.T.astype(bf16)
            return carry

        lax.fori_loop(0, per_block, turn, 0)
        v_copy(mb).wait_recv()

        def mix(gi, carry):
            v = (V[:, cols(gi)].astype(f32) + VR[mb, :, cols(gi)].astype(f32)).astype(bf16)
            cot = C[mb, :, cols(gi)].astype(f32)
            gm = (cot * X[mb, :, cols(gi)].astype(f32)).astype(bf16)
            conv = matmul(TC[gi], windows(jnp.concatenate([zero_block, v], axis=0)))
            for i in range(NT):
                part = slice(i * TB, (i + 1) * TB)
                G[part, cols(gi)] = (cot[part] * conv[:, i * gw : (i + 1) * gw]).astype(bf16)
            v_side = jnp.concatenate([v[i * TB : (i + 1) * TB] for i in range(NT)], axis=1)
            x = contract_last(v_side, windows(jnp.concatenate([gm, zero_block], axis=0)))
            n = TB
            while n > 1:
                half = n // 2
                x = x[:half] + pltpu.roll(x[half:n], 2 * TB - half, 1)
                n = half
            FG[pl.ds(gi, 1), :] = FG[pl.ds(gi, 1), :] + x[:, :TB]
            return carry

        lax.fori_loop(0, n_groups, mix, 0)

        for i in range(2):
            blk = pl.ds(pl.multiple_of((2 * i + 1 - c) * BW, BW), BW)
            pltpu.make_async_copy(
                GV.at[pl.ds(mb * TOK, TOK), blk], GV.at[pl.ds(mb * TOK, TOK), blk], gv_recv.at[mb, i]
            ).wait()

        def returned(j, carry):
            res = contract_last(GV[mb * TOK : (mb + 1) * TOK, :], W[pl.ds(pl.multiple_of(j * RN, RN), RN), :])
            at = cols(h * (BW // RN) + j, RN)
            G[:, at] = (G[:, at].astype(f32) + res).astype(bf16)
            return carry

        lax.fori_loop(0, BW // RN, returned, 0)

        def moment(gi, acc):
            return acc + G[:, cols(gi)].astype(f32) * X[mb, :, cols(gi)].astype(f32)

        PM[mb, 0] = lax.fori_loop(0, n_groups, moment, jnp.zeros((TOK, gw), f32))
        pm_copy(mb).start()
        pm_copy(mb).wait_recv()
        mean = jnp.sum(PM[mb, 0] + PM[mb, 1], axis=1, keepdims=True) / D
        PM[mb, 1] = jnp.broadcast_to(mean, (TOK, gw))
        keep = jnp.where(h == 0, 1.0, 0.0).astype(f32)

        def final(gi, carry):
            n = X[mb, :, cols(gi)].astype(f32)
            grad = R[mb] * (G[:, cols(gi)].astype(f32) - n * PM[mb, 1])
            OS[mb, :, cols(gi)] = (grad + keep * C[mb, :, cols(gi)].astype(f32)).astype(bf16)
            return carry

        lax.fori_loop(0, n_groups, final, 0)

    def out_blk(i):
        return pl.ds(pl.multiple_of((2 * i + c) * BW, BW), BW)

    def out_remote(mb, q, i):
        dst, sec = ((od_hbm, prev_s), (ou_hbm, up_s))[mb]
        return pltpu.make_async_remote_copy(
            src_ref=OS.at[mb, pl.ds(q * TB, TB), pl.ds(i * BW, BW)],
            dst_ref=dst.at[h, :, out_blk(i)],
            send_sem=o_send.at[mb, q, i], recv_sem=o_recv.at[mb, t, i],
            device_id=(sec, q), device_id_type=MESH,
        )

    def out_local(q, i):
        return pltpu.make_async_copy(
            OS.at[1, pl.ds(q * TB, TB), pl.ds(i * BW, BW)], ou_hbm.at[h, :, out_blk(i)], o_recv.at[1, q, i]
        )

    w_copy.wait()
    layer(0)
    v_copy(0).wait_send()
    gather_wait(1)
    for q in range(NT):
        for i in range(2):
            out_remote(0, q, i).start()
    layer(1)
    for q in range(NT):
        own = jnp.logical_and(up_self, t == q)
        for i in range(2):
            @pl.when(own)
            def _():
                out_local(q, i).start()

            @pl.when(jnp.logical_not(own))
            def _():
                out_remote(1, q, i).start()

    def fg_copy(q):
        return pltpu.make_async_remote_copy(
            src_ref=FG, dst_ref=fg_hbm.at[t], send_sem=fg_send.at[q], recv_sem=fg_recv.at[t],
            device_id=(s, q), device_id_type=MESH,
        )

    for q in range(NT):
        @pl.when(t != q)
        def _():
            fg_copy(q).start()

        @pl.when(t == q)
        def _():
            pltpu.make_async_copy(FG, fg_hbm.at[q], fg_recv.at[q]).start()

    DN = min(512, BW)
    tiles = D // DN

    def dw_copy(j, slot):
        return pltpu.make_async_copy(DW.at[slot], dw_hbm.at[:, cols(j, DN)], dw_sem.at[slot])

    def dw_tile(j, carry):
        slot = lax.rem(j, 2)

        @pl.when(j >= 2)
        def _():
            dw_copy(j - 2, slot).wait()

        DW[slot] = matmul(NBT[...], GV[:, cols(j, DN)]).astype(bf16)
        dw_copy(j, slot).start()
        return carry

    lax.fori_loop(0, tiles, dw_tile, 0)
    for j in (tiles - 2, tiles - 1):
        dw_copy(j, j % 2).wait()

    for arr in range(2):
        relay_copy(arr).wait_send()
    for q in range(NT):
        @pl.when(t != q)
        def _():
            for arr, (src, dst) in enumerate(((xd_hbm, X), (cd_hbm, C))):
                for i in range(2):
                    piece(src, dst, 0, arr, q, i, (s, q), t).wait_send()
            r_copy(0, q, (s, q)).wait_send()
            fg_copy(q).wait_send()

        for arr in range(2):
            for i in range(2):
                piece(U.at[arr], (X, C)[arr], 1, arr, q, i, (flip, q), t).wait_send()
        r_copy(1, q, (flip, q)).wait_send()
        pltpu.make_async_copy(FG, fg_hbm.at[q], fg_recv.at[q]).wait()
        own = jnp.logical_and(up_self, t == q)
        for i in range(2):
            out_remote(0, q, i).wait_send()

            @pl.when(jnp.logical_not(own))
            def _():
                out_remote(1, q, i).wait_send()
    v_copy(1).wait_send()
    for mb in range(2):
        pm_copy(mb).wait_send()
        for i in range(2):
            gv_copy(mb, i).wait_send()
    for mb, dst in enumerate((od_hbm, ou_hbm)):
        for q in range(NT):
            for i in range(2):
                landed = dst.at[q // 2, :, pl.ds((2 * i + q % 2) * BW, BW)]
                pltpu.make_async_copy(landed, landed, o_recv.at[mb, q, i]).wait()


def per_device(sections, weights, filters, down_input, down_cot, up_input, up_cot):
    w = weights[0]
    taps = filters[0]
    BW, D = w.shape
    TB = down_input.shape[1]
    CW = 2 * BW
    TOK = NT * TB
    groups, K = taps.shape
    n_groups = groups // 2
    hbm = pl.BlockSpec(memory_space=pl.ANY)
    dma = pltpu.SemaphoreType.DMA
    DN = min(512, BW)
    dw, fg, od, ou = pl.pallas_call(
        functools.partial(kernel, sections),
        out_shape=(
            jax.ShapeDtypeStruct((BW, D), bf16),
            jax.ShapeDtypeStruct((NT, n_groups, K), f32),
            jax.ShapeDtypeStruct((2, TB, D), bf16),
            jax.ShapeDtypeStruct((2, TB, D), bf16),
        ),
        in_specs=[hbm, pl.BlockSpec(memory_space=pltpu.VMEM), hbm, hbm, hbm, hbm],
        out_specs=(hbm, hbm, hbm, hbm),
        scratch_shapes=[
            pltpu.VMEM((BW, D), bf16),
            pltpu.VMEM((2, TOK, CW), bf16),
            pltpu.VMEM((2, TOK, CW), bf16),
            pltpu.VMEM((2, TOK, 128), f32),
            pltpu.VMEM((TB, D), bf16),
            pltpu.VMEM((2, TB, D), bf16),
            pltpu.VMEM((2, TB, 128), f32),
            pltpu.VMEM((n_groups, TB, 2 * TB), bf16),
            pltpu.VMEM((n_groups, TB, 2 * TB), bf16),
            pltpu.VMEM((BW, 2 * TOK), bf16),
            pltpu.VMEM((2 * TOK, D), bf16),
            pltpu.VMEM((TOK, CW), bf16),
            pltpu.VMEM((TOK, CW), bf16),
            pltpu.VMEM((2, TOK, CW), bf16),
            pltpu.VMEM((TOK, CW), bf16),
            pltpu.VMEM((2, 2, TOK, 128), f32),
            pltpu.VMEM((2, TOK, CW), bf16),
            pltpu.VMEM((n_groups, K), f32),
            pltpu.VMEM((2, BW, DN), bf16),
            dma((2, 2, NT, 2)), dma((2, 2, NT, 2)), dma((2, NT)), dma((2, NT)),
            dma((2,)), dma((2,)), dma((2,)), dma((2,)),
            dma((2, 2)), dma((2, 2)), dma((2,)), dma((2,)),
            dma((2, NT, 2)), dma((2, NT, 2)), dma((NT,)), dma((NT,)),
            dma, dma, dma((2,)),
        ],
        compiler_params=pltpu.CompilerParams(
            collective_id=0, has_side_effects=True, vmem_limit_bytes=60 * 1024 * 1024
        ),
        name="relay_backward",
    )(w, taps, down_input[0], down_cot[0], up_input[0], up_cot[0])
    s = lax.axis_index("section")
    down = od[0].astype(f32) + od[1].astype(f32)
    up = ou[0].astype(f32) + ou[1].astype(f32)
    down = jnp.where(s == sections - 1, 0.0, down).astype(bf16)
    up = jnp.where(s == 0, 0.0, up).astype(bf16)
    fg = fg.reshape(2, 2, 2, groups // NT, K)
    fg = jnp.transpose(fg[0] + fg[1], (1, 0, 2, 3)).reshape(groups, K)
    return dw[None], fg[None], down[None], up[None]


def solution(mesh):
    row = P("section", "tensor", None)
    whole = P("section", None, None)
    return jax.shard_map(
        functools.partial(per_device, mesh.shape["section"]),
        mesh=mesh,
        in_specs=(row, whole, row, row, row, row),
        out_specs=(row, whole, row, row),
        check_vma=False,
    )
```

```python
import functools

import jax
import jax.numpy as jnp
from jax import lax
from jax.experimental import pallas as pl
from jax.experimental.pallas import tpu as pltpu
from jax.sharding import PartitionSpec as P

epsilon = 1e-06
MESH = pl.DeviceIdType.MESH
bf16 = jnp.bfloat16
f32 = jnp.float32
NT = 4


def contract_last(a, b):
    return lax.dot_general(a, b, (((1,), (1,)), ((), ())), preferred_element_type=f32)


def matmul(a, b):
    return jnp.dot(a, b, preferred_element_type=f32)


def kernel(
    sections,
    w_hbm, f_ref, xd_hbm, cd_hbm, xu_hbm, cu_hbm,
    dw_hbm, fg_hbm, od_hbm, ou_hbm,
    W, X, C, R, OWN, U, RS, T, TC, NBT, GV, VS, V, VR, G, PM, OS, RB, FG, DW,
    g_send, g_recv, r_send, r_recv, u_send, u_recv, v_send, v_recv,
    gv_send, gv_recv, pm_send, pm_recv, o_send, o_recv, f_send, f_recv, fg_send, fg_recv,
    w_sem, own_sem, dw_sem,
):
    S = sections
    s = lax.axis_index("section")
    t = lax.axis_index("tensor")
    h = t // 2
    c = t % 2
    sib = (s, h * 2 + (1 - c))
    TB, D = xd_hbm.shape
    BW = D // NT
    CW = 2 * BW
    TOK = NT * TB
    groups = f_ref.shape[0]
    per_block = groups // NT
    n_groups = 2 * per_block
    gw = D // groups
    flip = s + 1 - 2 * (s % 2)
    mirror = S - 1 - s
    relay = mirror + 1 - 2 * (mirror % 2)
    odd = s % 2 == 1
    down_s = lax.rem(s + S - 2, S)
    up_s = lax.rem(S - s, S)
    up_self = up_s == s

    barrier = pltpu.get_barrier_semaphore()

    def greet(dev):
        pl.semaphore_signal(barrier, inc=1, device_id=dev, device_id_type=MESH)

    for q in range(1, NT):
        greet((s, lax.rem(t + q, NT)))
    greet((relay, t))
    for q in range(NT):
        greet((flip, q))

    @pl.when(odd)
    def _():
        greet((lax.rem(s + 2, S), t))

    @pl.when(jnp.logical_not(up_self))
    def _():
        greet((up_s, t))

    w_copy = pltpu.make_async_copy(w_hbm, W, w_sem)
    w_copy.start()
    own_copy = pltpu.make_async_copy(xd_hbm, OWN, own_sem)
    own_copy.start()
    pl.semaphore_wait(barrier, 8 + jnp.where(odd, 1, 0) + jnp.where(up_self, 0, 1))

    my_rows = pl.ds(pl.multiple_of(t * TB, TB), TB)

    def piece(src, dst_ref, mb, arr, q, i, dev, src_t):
        return pltpu.make_async_remote_copy(
            src_ref=src.at[:, pl.ds((2 * i + q % 2) * BW, BW)],
            dst_ref=dst_ref.at[mb, pl.ds(pl.multiple_of(src_t * TB, TB), TB), pl.ds(i * BW, BW)],
            send_sem=g_send.at[mb, arr, q, i],
            recv_sem=g_recv.at[mb, arr, src_t, i],
            device_id=dev,
            device_id_type=MESH,
        )

    def local_piece(src, dst_ref, mb, arr, q, i):
        return pltpu.make_async_copy(
            src.at[:, pl.ds((2 * i + q % 2) * BW, BW)],
            dst_ref.at[mb, pl.ds(q * TB, TB), pl.ds(i * BW, BW)],
            g_recv.at[mb, arr, q, i],
        )

    for arr, (src, dst) in enumerate(((xd_hbm, X), (cd_hbm, C))):
        for q in range(NT):
            @pl.when(t != q)
            def _():
                for i in range(2):
                    piece(src, dst, 0, arr, q, i, (s, q), t).start()

            @pl.when(t == q)
            def _():
                for i in range(2):
                    local_piece(src, dst, 0, arr, q, i).start()

    def relay_copy(arr):
        return pltpu.make_async_remote_copy(
            src_ref=(xu_hbm, cu_hbm)[arr], dst_ref=U.at[arr],
            send_sem=u_send.at[arr], recv_sem=u_recv.at[arr],
            device_id=(relay, t), device_id_type=MESH,
        )

    for arr in range(2):
        relay_copy(arr).start()

    def inverse_rms(ref):
        def step(j, acc):
            x = ref[:, pl.ds(pl.multiple_of(j * gw, gw), gw)].astype(f32)
            return acc + x * x
        acc = lax.fori_loop(0, D // gw, step, jnp.zeros((TB, gw), f32))
        mean = jnp.sum(acc, axis=1, keepdims=True) / D
        return jnp.broadcast_to(lax.rsqrt(mean + epsilon), (TB, 128))

    def r_copy(mb, q, dev):
        return pltpu.make_async_remote_copy(
            src_ref=RS.at[mb], dst_ref=R.at[mb, my_rows, :],
            send_sem=r_send.at[mb, q], recv_sem=r_recv.at[mb, t],
            device_id=dev, device_id_type=MESH,
        )

    own_copy.wait()
    RS[0] = inverse_rms(OWN)
    for q in range(NT):
        @pl.when(t != q)
        def _():
            r_copy(0, q, (s, q)).start()

        @pl.when(t == q)
        def _():
            R[0, q * TB : (q + 1) * TB, :] = RS[0]

    rows = lax.broadcasted_iota(jnp.int32, (TB, 2 * TB), 0)

    def build(gi, carry):
        g = (gi // per_block * 2 + c) * per_block + lax.rem(gi, per_block)
        taps = jnp.broadcast_to(f_ref[pl.ds(g, 1), :], (TB, TB))
        x = jnp.concatenate([taps, jnp.zeros((TB, TB), f32)], axis=1)
        step = 1
        while step < TB:
            x = jnp.where((rows & step) != 0, pltpu.roll(x, step, 1), x)
            step *= 2
        T[gi] = x.astype(bf16)
        TC[gi] = jnp.concatenate([x[:, TB:].T, x[:, :TB].T], axis=1).astype(bf16)
        return carry

    lax.fori_loop(0, n_groups, build, 0)
    FG[...] = jnp.zeros_like(FG)

    def gather_wait(mb):
        for arr, dst in enumerate((X, C)):
            for q in range(NT):
                for i in range(2):
                    pltpu.make_async_copy(
                        dst.at[mb, pl.ds(q * TB, TB), pl.ds(i * BW, BW)],
                        dst.at[mb, pl.ds(q * TB, TB), pl.ds(i * BW, BW)],
                        g_recv.at[mb, arr, q, i],
                    ).wait()
        for q in range(NT):
            def wait_r():
                pltpu.make_async_copy(RS.at[mb], R.at[mb, pl.ds(q * TB, TB), :], r_recv.at[mb, q]).wait()
            if mb == 0:
                pl.when(t != q)(wait_r)
            else:
                wait_r()

    gather_wait(0)

    for arr in range(2):
        relay_copy(arr).wait_recv()
        for q in range(NT):
            for i in range(2):
                piece(U.at[arr], (X, C)[arr], 1, arr, q, i, (flip, q), t).start()
    RS[1] = inverse_rms(U.at[0])
    for q in range(NT):
        r_copy(1, q, (flip, q)).start()

    def cols(j, width=gw):
        return pl.ds(pl.multiple_of(j * width, width), width)

    def natural(gi):
        return (gi // per_block * 2 + c) * per_block + lax.rem(gi, per_block)

    def windows(x):
        return jnp.concatenate([x[i * TB : (i + 2) * TB] for i in range(NT)], axis=1)

    zero_block = jnp.zeros((TB, gw), bf16)

    def gv_copy(mb, i):
        blk = pl.ds(pl.multiple_of((2 * i + c) * BW, BW), BW)
        return pltpu.make_async_remote_copy(
            src_ref=GV.at[pl.ds(mb * TOK, TOK), blk], dst_ref=GV.at[pl.ds(mb * TOK, TOK), blk],
            send_sem=gv_send.at[mb, i], recv_sem=gv_recv.at[mb, i],
            device_id=sib, device_id_type=MESH,
        )

    def v_copy(mb):
        return pltpu.make_async_remote_copy(
            src_ref=VS, dst_ref=VR.at[mb],
            send_sem=v_send.at[mb], recv_sem=v_recv.at[mb],
            device_id=sib, device_id_type=MESH,
        )

    def pm_copy(mb):
        return pltpu.make_async_remote_copy(
            src_ref=PM.at[mb, 0], dst_ref=PM.at[mb, 1],
            send_sem=pm_send.at[mb], recv_sem=pm_recv.at[mb],
            device_id=sib, device_id_type=MESH,
        )

    VN = min(512, BW)
    RN = min(256, BW)

    def layer(mb, between):
        def prep(gi, carry):
            n = X[mb, :, cols(gi)].astype(f32) * R[mb]
            gm = (C[mb, :, cols(gi)].astype(f32) * n).astype(bf16)
            X[mb, :, cols(gi)] = n.astype(bf16)
            w = windows(jnp.concatenate([gm, zero_block], axis=0))
            gv = matmul(T[gi], w).astype(bf16)
            for i in range(NT):
                GV[mb * TOK + i * TB : mb * TOK + (i + 1) * TB, cols(natural(gi))] = gv[:, i * gw : (i + 1) * gw]
            return carry

        lax.fori_loop(0, n_groups, prep, 0)
        for i in range(2):
            gv_copy(mb, i).start()

        own_cols = pl.ds(pl.multiple_of(h * BW, BW), BW)

        def sib_values(j, carry):
            src = (j // (BW // VN) * 2 + (1 - c)) * (BW // VN) + lax.rem(j, BW // VN)
            VS[:, cols(j, VN)] = matmul(X[mb, :, own_cols], W[:, cols(src, VN)]).astype(bf16)
            return carry

        def own_values(j, carry):
            src = (j // (BW // VN) * 2 + c) * (BW // VN) + lax.rem(j, BW // VN)
            V[:, cols(j, VN)] = matmul(X[mb, :, own_cols], W[:, cols(src, VN)]).astype(bf16)
            return carry

        lax.fori_loop(0, CW // VN, sib_values, 0)
        v_copy(mb).start()
        lax.fori_loop(0, CW // VN, own_values, 0)

        def turn(j, carry):
            n = X[mb, :, cols(h * per_block + j)].astype(f32)
            NBT[cols(j), mb * TOK : (mb + 1) * TOK] = n.T.astype(bf16)
            return carry

        lax.fori_loop(0, per_block, turn, 0)
        v_copy(mb).wait_recv()

        def mix(gi, carry):
            v = (V[:, cols(gi)].astype(f32) + VR[mb, :, cols(gi)].astype(f32)).astype(bf16)
            cot = C[mb, :, cols(gi)].astype(f32)
            gm = (cot * X[mb, :, cols(gi)].astype(f32)).astype(bf16)
            conv = matmul(TC[gi], windows(jnp.concatenate([zero_block, v], axis=0)))
            for i in range(NT):
                part = slice(i * TB, (i + 1) * TB)
                G[part, cols(gi)] = (cot[part] * conv[:, i * gw : (i + 1) * gw]).astype(bf16)
            v_side = jnp.concatenate([v[i * TB : (i + 1) * TB] for i in range(NT)], axis=1)
            x = contract_last(v_side, windows(jnp.concatenate([gm, zero_block], axis=0)))
            n = TB
            while n > 1:
                half = n // 2
                x = x[:half] + pltpu.roll(x[half:n], 2 * TB - half, 1)
                n = half
            FG[pl.ds(gi, 1), :] = FG[pl.ds(gi, 1), :] + x[:, :TB]
            return carry

        lax.fori_loop(0, n_groups, mix, 0)

        if between is not None:
            between(0, 0)
        for i in range(2):
            blk = pl.ds(pl.multiple_of((2 * i + 1 - c) * BW, BW), BW)
            pltpu.make_async_copy(
                GV.at[pl.ds(mb * TOK, TOK), blk], GV.at[pl.ds(mb * TOK, TOK), blk], gv_recv.at[mb, i]
            ).wait()

        def returned(j, carry):
            res = contract_last(GV[mb * TOK : (mb + 1) * TOK, :], W[pl.ds(pl.multiple_of(j * RN, RN), RN), :])
            at = cols(h * (BW // RN) + j, RN)
            G[:, at] = (G[:, at].astype(f32) + res).astype(bf16)
            return carry

        lax.fori_loop(0, BW // RN, returned, 0)
        if between is not None:
            between(0, 1)

        def moment(gi, acc):
            return acc + G[:, cols(gi)].astype(f32) * X[mb, :, cols(gi)].astype(f32)

        PM[mb, 0] = lax.fori_loop(0, n_groups, moment, jnp.zeros((TOK, gw), f32))
        pm_copy(mb).start()
        pm_copy(mb).wait_recv()
        mean = jnp.sum(PM[mb, 0] + PM[mb, 1], axis=1, keepdims=True) / D
        PM[mb, 1] = jnp.broadcast_to(mean, (TOK, gw))
        keep = jnp.where(h == 0, 1.0, 0.0).astype(f32)

        def final(gi, carry):
            n = X[mb, :, cols(gi)].astype(f32)
            grad = R[mb] * (G[:, cols(gi)].astype(f32) - n * PM[mb, 1])
            OS[mb, :, cols(gi)] = (grad + keep * C[mb, :, cols(gi)].astype(f32)).astype(bf16)
            return carry

        lax.fori_loop(0, n_groups, final, 0)

    HB = TB // 2
    CHUNKS = 4

    def out_src(mb, q, k):
        return OS.at[mb, pl.ds(q * TB + k % 2 * HB, HB), pl.ds(k // 2 * BW, BW)]

    def out_dst(mb, k):
        blk = pl.ds(pl.multiple_of((k // 2 * 2 + c) * BW, BW), BW)
        return RB.at[mb, h, pl.ds(k % 2 * HB, HB), blk]

    def out_remote(mb, q, k):
        return pltpu.make_async_remote_copy(
            src_ref=out_src(mb, q, k), dst_ref=out_dst(mb, k),
            send_sem=o_send.at[mb, q, k], recv_sem=o_recv.at[mb, t, k],
            device_id=((flip, s)[mb], q), device_id_type=MESH,
        )

    def out_start(mb, k):
        for q in range(NT):
            if mb == 0:
                out_remote(mb, q, k).start()
            else:
                @pl.when(t != q)
                def _():
                    out_remote(mb, q, k).start()

                @pl.when(t == q)
                def _():
                    pltpu.make_async_copy(out_src(mb, q, k), out_dst(mb, k), o_recv.at[mb, q, k]).start()

    def out_sent(mb, k):
        for q in range(NT):
            if mb == 0:
                out_remote(mb, q, k).wait_send()
            else:
                @pl.when(t != q)
                def _():
                    out_remote(mb, q, k).wait_send()

    def sum_area(k):
        return pl.ds(k % 2 * HB, HB), pl.ds(k // 2 * 2 * BW, 2 * BW)

    def final_dst(mb, k):
        return (od_hbm, ou_hbm)[mb].at[sum_area(k)]

    def final_remote(mb, k):
        return pltpu.make_async_remote_copy(
            src_ref=U.at[(mb,) + sum_area(k)], dst_ref=final_dst(mb, k),
            send_sem=f_send.at[mb, k], recv_sem=f_recv.at[mb, k],
            device_id=((down_s, up_s)[mb], t), device_id_type=MESH,
        )

    def goes(mb):
        return odd if mb == 0 else jnp.logical_not(up_self)

    def relay_step(mb, k):
        rows_k, cols_k = sum_area(k)
        for q in range(NT):
            blk = pl.ds((k // 2 * 2 + q % 2) * BW, BW)
            landed = RB.at[mb, q // 2, rows_k, blk]
            pltpu.make_async_copy(landed, landed, o_recv.at[mb, q, k]).wait()
        total = RB[mb, 0, rows_k, cols_k].astype(f32) + RB[mb, 1, rows_k, cols_k].astype(f32)
        first = (flip, s)[mb] == 0
        U[(mb,) + sum_area(k)] = jnp.where(first, 0.0, total).astype(bf16)

        @pl.when(goes(mb))
        def _():
            final_remote(mb, k).start()

        @pl.when(jnp.logical_not(goes(mb)))
        def _():
            pltpu.make_async_copy(U.at[(mb,) + sum_area(k)], final_dst(mb, k), f_recv.at[mb, k]).start()

    def forwards_sent():
        for arr in range(2):
            for q in range(NT):
                for i in range(2):
                    piece(U.at[arr], (X, C)[arr], 1, arr, q, i, (flip, q), t).wait_send()
        for q in range(NT):
            r_copy(1, q, (flip, q)).wait_send()

    w_copy.wait()
    layer(0, None)
    v_copy(0).wait_send()
    gather_wait(1)
    for k in range(CHUNKS):
        out_start(0, k)
    forwards_sent()
    layer(1, relay_step)
    out_start(1, 0)
    out_start(1, 1)

    def fg_copy(q):
        return pltpu.make_async_remote_copy(
            src_ref=FG, dst_ref=fg_hbm.at[t], send_sem=fg_send.at[q], recv_sem=fg_recv.at[t],
            device_id=(s, q), device_id_type=MESH,
        )

    for q in range(NT):
        @pl.when(t != q)
        def _():
            fg_copy(q).start()

        @pl.when(t == q)
        def _():
            pltpu.make_async_copy(FG, fg_hbm.at[q], fg_recv.at[q]).start()

    DN = min(512, BW)
    tiles = D // DN

    def dw_copy(j, slot):
        return pltpu.make_async_copy(DW.at[slot], dw_hbm.at[:, cols(j, DN)], dw_sem.at[slot])

    def dw_tile(j, carry):
        slot = lax.rem(j, 2)

        @pl.when(j >= 2)
        def _():
            dw_copy(j - 2, slot).wait()

        DW[slot] = matmul(NBT[...], GV[:, cols(j, DN)]).astype(bf16)
        dw_copy(j, slot).start()
        return carry

    for k in range(CHUNKS):
        lax.fori_loop(k * tiles // CHUNKS, (k + 1) * tiles // CHUNKS, dw_tile, 0)
        if k < 2:
            relay_step(0, k + 2)
        if k + 2 < CHUNKS:
            out_sent(1, k)
            out_start(1, k + 2)
        relay_step(1, k)
    for j in (tiles - 2, tiles - 1):
        dw_copy(j, j % 2).wait()

    for arr in range(2):
        relay_copy(arr).wait_send()
    for q in range(NT):
        @pl.when(t != q)
        def _():
            for arr, (src, dst) in enumerate(((xd_hbm, X), (cd_hbm, C))):
                for i in range(2):
                    piece(src, dst, 0, arr, q, i, (s, q), t).wait_send()
            r_copy(0, q, (s, q)).wait_send()
            fg_copy(q).wait_send()

        pltpu.make_async_copy(FG, fg_hbm.at[q], fg_recv.at[q]).wait()
    for k in range(CHUNKS):
        out_sent(0, k)
        if k >= CHUNKS - 2:
            out_sent(1, k)
    v_copy(1).wait_send()
    for mb in range(2):
        pm_copy(mb).wait_send()
        for i in range(2):
            gv_copy(mb, i).wait_send()
    for mb in range(2):
        for k in range(CHUNKS):
            @pl.when(goes(mb))
            def _():
                final_remote(mb, k).wait_send()

            pltpu.make_async_copy(final_dst(mb, k), final_dst(mb, k), f_recv.at[mb, k]).wait()


def per_device(sections, weights, filters, down_input, down_cot, up_input, up_cot):
    w = weights[0]
    taps = filters[0]
    BW, D = w.shape
    TB = down_input.shape[1]
    CW = 2 * BW
    TOK = NT * TB
    groups, K = taps.shape
    n_groups = groups // 2
    hbm = pl.BlockSpec(memory_space=pl.ANY)
    dma = pltpu.SemaphoreType.DMA
    DN = min(512, BW)
    dw, fg, od, ou = pl.pallas_call(
        functools.partial(kernel, sections),
        out_shape=(
            jax.ShapeDtypeStruct((BW, D), bf16),
            jax.ShapeDtypeStruct((NT, n_groups, K), f32),
            jax.ShapeDtypeStruct((TB, D), bf16),
            jax.ShapeDtypeStruct((TB, D), bf16),
        ),
        in_specs=[hbm, pl.BlockSpec(memory_space=pltpu.VMEM), hbm, hbm, hbm, hbm],
        out_specs=(hbm, hbm, hbm, hbm),
        scratch_shapes=[
            pltpu.VMEM((BW, D), bf16),
            pltpu.VMEM((2, TOK, CW), bf16),
            pltpu.VMEM((2, TOK, CW), bf16),
            pltpu.VMEM((2, TOK, 128), f32),
            pltpu.VMEM((TB, D), bf16),
            pltpu.VMEM((2, TB, D), bf16),
            pltpu.VMEM((2, TB, 128), f32),
            pltpu.VMEM((n_groups, TB, 2 * TB), bf16),
            pltpu.VMEM((n_groups, TB, 2 * TB), bf16),
            pltpu.VMEM((BW, 2 * TOK), bf16),
            pltpu.VMEM((2 * TOK, D), bf16),
            pltpu.VMEM((TOK, CW), bf16),
            pltpu.VMEM((TOK, CW), bf16),
            pltpu.VMEM((2, TOK, CW), bf16),
            pltpu.VMEM((TOK, CW), bf16),
            pltpu.VMEM((2, 2, TOK, 128), f32),
            pltpu.VMEM((2, TOK, CW), bf16),
            pltpu.VMEM((2, 2, TB, D), bf16),
            pltpu.VMEM((n_groups, K), f32),
            pltpu.VMEM((2, BW, DN), bf16),
            dma((2, 2, NT, 2)), dma((2, 2, NT, 2)), dma((2, NT)), dma((2, NT)),
            dma((2,)), dma((2,)), dma((2,)), dma((2,)),
            dma((2, 2)), dma((2, 2)), dma((2,)), dma((2,)),
            dma((2, NT, 4)), dma((2, NT, 4)), dma((2, 4)), dma((2, 4)), dma((NT,)), dma((NT,)),
            dma, dma, dma((2,)),
        ],
        compiler_params=pltpu.CompilerParams(
            collective_id=0, has_side_effects=True, vmem_limit_bytes=60 * 1024 * 1024
        ),
        name="relay_backward",
    )(w, taps, down_input[0], down_cot[0], up_input[0], up_cot[0])
    fg = fg.reshape(2, 2, 2, groups // NT, K)
    fg = jnp.transpose(fg[0] + fg[1], (1, 0, 2, 3)).reshape(groups, K)
    return dw[None], fg[None], od[None], ou[None]


def solution(mesh):
    row = P("section", "tensor", None)
    whole = P("section", None, None)
    return jax.shard_map(
        functools.partial(per_device, mesh.shape["section"]),
        mesh=mesh,
        in_specs=(row, whole, row, row, row, row),
        out_specs=(row, whole, row, row),
        check_vma=False,
    )
```

```python
import functools

import jax
import jax.numpy as jnp
from jax import lax
from jax.experimental import pallas as pl
from jax.experimental.pallas import tpu as pltpu
from jax.sharding import PartitionSpec as P

epsilon = 1e-06
MESH = pl.DeviceIdType.MESH
bf16 = jnp.bfloat16
f32 = jnp.float32
NT = 4


def contract_last(a, b):
    return lax.dot_general(a, b, (((1,), (1,)), ((), ())), preferred_element_type=f32)


def matmul(a, b):
    return jnp.dot(a, b, preferred_element_type=f32)


def kernel(
    sections,
    w_hbm, f_ref, xd_hbm, cd_hbm, xu_hbm, cu_hbm,
    dw_hbm, fg_hbm, od_hbm, ou_hbm,
    W, X, C, R, OWN, U, RS, T, TC, NBT, GV, VS, V, VR, G, PM, OS, RB, PAIRS, FG, DW,
    g_send, g_recv, r_send, r_recv, u_send, u_recv, v_send, v_recv,
    gv_send, gv_recv, pm_send, pm_recv, o_send, o_recv, f_send, f_recv, fg_send, fg_recv,
    w_sem, own_sem, dw_sem,
):
    S = sections
    s = lax.axis_index("section")
    t = lax.axis_index("tensor")
    h = t // 2
    c = t % 2
    sib = (s, h * 2 + (1 - c))
    TB, D = xd_hbm.shape
    BW = D // NT
    CW = 2 * BW
    TOK = NT * TB
    groups = f_ref.shape[0]
    per_block = groups // NT
    n_groups = 2 * per_block
    gw = D // groups
    flip = s + 1 - 2 * (s % 2)
    mirror = S - 1 - s
    relay = mirror + 1 - 2 * (mirror % 2)
    odd = s % 2 == 1
    down_s = lax.rem(s + S - 2, S)
    up_s = lax.rem(S - s, S)
    up_self = up_s == s

    barrier = pltpu.get_barrier_semaphore()

    def greet(dev):
        pl.semaphore_signal(barrier, inc=1, device_id=dev, device_id_type=MESH)

    for q in range(1, NT):
        greet((s, lax.rem(t + q, NT)))
    greet((relay, t))
    for q in range(NT):
        greet((flip, q))

    @pl.when(odd)
    def _():
        greet((lax.rem(s + 2, S), t))

    @pl.when(jnp.logical_not(up_self))
    def _():
        greet((up_s, t))

    w_copy = pltpu.make_async_copy(w_hbm, W, w_sem)
    w_copy.start()
    own_copy = pltpu.make_async_copy(xd_hbm, OWN, own_sem)
    own_copy.start()
    pl.semaphore_wait(barrier, 8 + jnp.where(odd, 1, 0) + jnp.where(up_self, 0, 1))

    my_rows = pl.ds(pl.multiple_of(t * TB, TB), TB)

    def piece(src, dst_ref, mb, arr, q, i, dev, src_t):
        return pltpu.make_async_remote_copy(
            src_ref=src.at[:, pl.ds((2 * i + q % 2) * BW, BW)],
            dst_ref=dst_ref.at[mb, pl.ds(pl.multiple_of(src_t * TB, TB), TB), pl.ds(i * BW, BW)],
            send_sem=g_send.at[mb, arr, q, i],
            recv_sem=g_recv.at[mb, arr, src_t, i],
            device_id=dev,
            device_id_type=MESH,
        )

    def local_piece(src, dst_ref, mb, arr, q, i):
        return pltpu.make_async_copy(
            src.at[:, pl.ds((2 * i + q % 2) * BW, BW)],
            dst_ref.at[mb, pl.ds(q * TB, TB), pl.ds(i * BW, BW)],
            g_recv.at[mb, arr, q, i],
        )

    def gather_start(arr):
        src, dst = ((xd_hbm, X), (cd_hbm, C))[arr]
        for q in range(NT):
            @pl.when(t != q)
            def _():
                for i in range(2):
                    piece(src, dst, 0, arr, q, i, (s, q), t).start()

            @pl.when(t == q)
            def _():
                for i in range(2):
                    local_piece(src, dst, 0, arr, q, i).start()

    def relay_copy(arr):
        return pltpu.make_async_remote_copy(
            src_ref=(xu_hbm, cu_hbm)[arr], dst_ref=U.at[arr],
            send_sem=u_send.at[arr], recv_sem=u_recv.at[arr],
            device_id=(relay, t), device_id_type=MESH,
        )

    gather_start(0)
    relay_copy(0).start()

    def inverse_rms(ref):
        def step(j, acc):
            x = ref[:, pl.ds(pl.multiple_of(j * gw, gw), gw)].astype(f32)
            return acc + x * x
        acc = lax.fori_loop(0, D // gw, step, jnp.zeros((TB, gw), f32))
        mean = jnp.sum(acc, axis=1, keepdims=True) / D
        return jnp.broadcast_to(lax.rsqrt(mean + epsilon), (TB, 128))

    def r_copy(mb, q, dev):
        return pltpu.make_async_remote_copy(
            src_ref=RS.at[mb], dst_ref=R.at[mb, my_rows, :],
            send_sem=r_send.at[mb, q], recv_sem=r_recv.at[mb, t],
            device_id=dev, device_id_type=MESH,
        )

    own_copy.wait()
    RS[0] = inverse_rms(OWN)
    for q in range(NT):
        @pl.when(t != q)
        def _():
            r_copy(0, q, (s, q)).start()

        @pl.when(t == q)
        def _():
            R[0, q * TB : (q + 1) * TB, :] = RS[0]

    rows = lax.broadcasted_iota(jnp.int32, (TB, 2 * TB), 0)

    def build(gi, carry):
        g = (gi // per_block * 2 + c) * per_block + lax.rem(gi, per_block)
        taps = jnp.broadcast_to(f_ref[pl.ds(g, 1), :], (TB, TB))
        x = jnp.concatenate([taps, jnp.zeros((TB, TB), f32)], axis=1)
        step = 1
        while step < TB:
            x = jnp.where((rows & step) != 0, pltpu.roll(x, step, 1), x)
            step *= 2
        T[gi] = x.astype(bf16)
        TC[gi] = jnp.concatenate([x[:, TB:].T, x[:, :TB].T], axis=1).astype(bf16)
        return carry

    lax.fori_loop(0, n_groups, build, 0)
    relay_copy(0).wait_send()
    gather_start(1)
    relay_copy(1).start()

    def gather_wait(mb, arr):
        dst = (X, C)[arr]
        for q in range(NT):
            for i in range(2):
                landed = dst.at[mb, pl.ds(q * TB, TB), pl.ds(i * BW, BW)]
                pltpu.make_async_copy(landed, landed, g_recv.at[mb, arr, q, i]).wait()

    def r_wait(mb):
        for q in range(NT):
            def wait_r():
                pltpu.make_async_copy(RS.at[mb], R.at[mb, pl.ds(q * TB, TB), :], r_recv.at[mb, q]).wait()
            if mb == 0:
                pl.when(t != q)(wait_r)
            else:
                wait_r()

    def forward(arr):
        for q in range(NT):
            for i in range(2):
                piece(U.at[arr], (X, C)[arr], 1, arr, q, i, (flip, q), t).start()

    def forward_sent(arr):
        for q in range(NT):
            for i in range(2):
                piece(U.at[arr], (X, C)[arr], 1, arr, q, i, (flip, q), t).wait_send()

    def cols(j, width=gw):
        return pl.ds(pl.multiple_of(j * width, width), width)

    def natural(gi):
        return (gi // per_block * 2 + c) * per_block + lax.rem(gi, per_block)

    def windows(x):
        return jnp.concatenate([x[i * TB : (i + 2) * TB] for i in range(NT)], axis=1)

    zero_block = jnp.zeros((TB, gw), bf16)

    def gv_copy(mb, i):
        blk = pl.ds(pl.multiple_of((2 * i + c) * BW, BW), BW)
        return pltpu.make_async_remote_copy(
            src_ref=GV.at[pl.ds(mb * TOK, TOK), blk], dst_ref=GV.at[pl.ds(mb * TOK, TOK), blk],
            send_sem=gv_send.at[mb, i], recv_sem=gv_recv.at[mb, i],
            device_id=sib, device_id_type=MESH,
        )

    def v_copy(mb):
        return pltpu.make_async_remote_copy(
            src_ref=VS, dst_ref=VR.at[mb],
            send_sem=v_send.at[mb], recv_sem=v_recv.at[mb],
            device_id=sib, device_id_type=MESH,
        )

    def pm_copy(mb):
        return pltpu.make_async_remote_copy(
            src_ref=PM.at[mb, 0], dst_ref=PM.at[mb, 1],
            send_sem=pm_send.at[mb], recv_sem=pm_recv.at[mb],
            device_id=sib, device_id_type=MESH,
        )

    VN = min(512, BW)
    RN = min(256, BW)
    UN = 2
    wide = min(512, BW)
    own_cols = pl.ds(pl.multiple_of(h * BW, BW), BW)

    def blocks(x):
        return [x[i * TB : (i + 1) * TB] for i in range(NT)]

    def values(mb):
        def norm(gi, carry):
            at = cols(gi, 2 * gw)
            scale = jnp.concatenate([R[mb], R[mb]], axis=1)
            X[mb, :, at] = (X[mb, :, at].astype(f32) * scale).astype(bf16)
            return carry

        lax.fori_loop(0, n_groups // 2, norm, 0)

        def sib_values(j, carry):
            src = (j // (BW // VN) * 2 + (1 - c)) * (BW // VN) + lax.rem(j, BW // VN)
            VS[:, cols(j, VN)] = matmul(X[mb, :, own_cols], W[:, cols(src, VN)]).astype(bf16)
            return carry

        def own_values(j, carry):
            src = (j // (BW // VN) * 2 + c) * (BW // VN) + lax.rem(j, BW // VN)
            V[:, cols(j, VN)] = matmul(X[mb, :, own_cols], W[:, cols(src, VN)]).astype(bf16)
            return carry

        lax.fori_loop(0, CW // VN, sib_values, 0)
        v_copy(mb).start()
        lax.fori_loop(0, CW // VN, own_values, 0)

        def turn(j, carry):
            n = X[mb, :, cols(h * per_block + j)].astype(f32)
            NBT[cols(j), mb * TOK : (mb + 1) * TOK] = n.T.astype(bf16)
            return carry

        lax.fori_loop(0, per_block, turn, 0)

    def mixed_grad(mb, gi):
        gm = C[mb, :, cols(gi)].astype(f32) * X[mb, :, cols(gi)].astype(f32)
        return windows(jnp.concatenate([gm.astype(bf16), zero_block], axis=0))

    def grads(mb):
        def grad(j, carry):
            gs = [j * UN + u for u in range(UN)]
            ws = [mixed_grad(mb, gi) for gi in gs]
            gvs = [matmul(T[gi], w).astype(bf16) for gi, w in zip(gs, ws)]
            for gi, gv in zip(gs, gvs):
                for i in range(NT):
                    GV[mb * TOK + i * TB : mb * TOK + (i + 1) * TB, cols(natural(gi))] = gv[:, i * gw : (i + 1) * gw]
            return carry

        lax.fori_loop(0, n_groups // UN, grad, 0)
        for i in range(2):
            gv_copy(mb, i).start()

    def convolve(mb):
        v_copy(mb).wait_recv()

        def mix(j, carry):
            gs = [j * UN + u for u in range(UN)]
            vs = [(V[:, cols(gi)].astype(f32) + VR[mb, :, cols(gi)].astype(f32)).astype(bf16) for gi in gs]
            cots = [C[mb, :, cols(gi)].astype(f32) for gi in gs]
            convs = [matmul(TC[gi], windows(jnp.concatenate([zero_block, v], axis=0))) for gi, v in zip(gs, vs)]
            for gi, v, cot, conv in zip(gs, vs, cots, convs):
                VR[mb, :, cols(gi)] = v
                conv = jnp.concatenate([conv[:, i * gw : (i + 1) * gw] for i in range(NT)], axis=0)
                G[:, cols(gi)] = (cot * conv).astype(bf16)
            return carry

        lax.fori_loop(0, n_groups // UN, mix, 0)

    def back(mb):
        for i in range(2):
            blk = pl.ds(pl.multiple_of((2 * i + 1 - c) * BW, BW), BW)
            landed = GV.at[pl.ds(mb * TOK, TOK), blk]
            pltpu.make_async_copy(landed, landed, gv_recv.at[mb, i]).wait()

        def returned(j, carry):
            res = contract_last(GV[mb * TOK : (mb + 1) * TOK, :], W[pl.ds(pl.multiple_of(j * RN, RN), RN), :])
            at = cols(h * (BW // RN) + j, RN)
            G[:, at] = (G[:, at].astype(f32) + res).astype(bf16)
            return carry

        lax.fori_loop(0, BW // RN, returned, 0)

    def finish(mb):
        def moment(j, acc):
            at = cols(j, wide)
            x = G[:, at].astype(f32) * X[mb, :, at].astype(f32)
            return acc + sum(x[:, i * gw : (i + 1) * gw] for i in range(wide // gw))

        PM[mb, 0] = lax.fori_loop(0, CW // wide, moment, jnp.zeros((TOK, gw), f32))
        pm_copy(mb).start()
        pm_copy(mb).wait_recv()
        mean = jnp.sum(PM[mb, 0] + PM[mb, 1], axis=1, keepdims=True) / D
        PM[mb, 1] = jnp.broadcast_to(mean, (TOK, gw))
        keep = jnp.where(h == 0, 1.0, 0.0).astype(f32)

        def final(j, carry):
            at = cols(j, 2 * gw)
            scale = jnp.concatenate([R[mb], R[mb]], axis=1)
            pm = jnp.concatenate([PM[mb, 1], PM[mb, 1]], axis=1)
            grad = scale * (G[:, at].astype(f32) - X[mb, :, at].astype(f32) * pm)
            OS[mb, :, at] = (grad + keep * C[mb, :, at].astype(f32)).astype(bf16)
            return carry

        lax.fori_loop(0, n_groups // 2, final, 0)

    def tap_pairs(mb):
        def pairs(j, carry):
            gs = [j * UN + u for u in range(UN)]
            ws = [mixed_grad(mb, gi) for gi in gs]
            vs = [jnp.concatenate(blocks(VR[mb, :, cols(gi)]), axis=1) for gi in gs]
            ps = [contract_last(v, w) for v, w in zip(vs, ws)]
            for gi, p in zip(gs, ps):
                PAIRS[gi] = p if mb == 0 else PAIRS[gi] + p
            return carry

        lax.fori_loop(0, n_groups // UN, pairs, 0)

    def tap_sums():
        n = TB
        while n > 8:
            half = n // 2
            for gi in range(n_groups):
                PAIRS[gi, :half] = PAIRS[gi, :half] + pltpu.roll(PAIRS[gi, half:n], 2 * TB - half, 1)
            n = half
        for gi in range(n_groups):
            x = PAIRS[gi, :8]
            for half in (4, 2, 1):
                x = x[:half] + pltpu.roll(x[half:], 2 * TB - half, 1)
            FG[gi : gi + 1, :] = x[:, :TB]

    HB = TB // 2
    CHUNKS = 4

    def out_src(mb, q, k):
        return OS.at[mb, pl.ds(q * TB + k % 2 * HB, HB), pl.ds(k // 2 * BW, BW)]

    def out_dst(mb, k):
        blk = pl.ds(pl.multiple_of((k // 2 * 2 + c) * BW, BW), BW)
        return RB.at[mb, h, pl.ds(k % 2 * HB, HB), blk]

    def out_remote(mb, q, k):
        return pltpu.make_async_remote_copy(
            src_ref=out_src(mb, q, k), dst_ref=out_dst(mb, k),
            send_sem=o_send.at[mb, q, k], recv_sem=o_recv.at[mb, t, k],
            device_id=((flip, s)[mb], q), device_id_type=MESH,
        )

    def out_start(mb, k):
        for q in range(NT):
            if mb == 0:
                out_remote(mb, q, k).start()
            else:
                @pl.when(t != q)
                def _():
                    out_remote(mb, q, k).start()

                @pl.when(t == q)
                def _():
                    pltpu.make_async_copy(out_src(mb, q, k), out_dst(mb, k), o_recv.at[mb, q, k]).start()

    def out_sent(mb, k):
        for q in range(NT):
            if mb == 0:
                out_remote(mb, q, k).wait_send()
            else:
                @pl.when(t != q)
                def _():
                    out_remote(mb, q, k).wait_send()

    def sum_area(k):
        return pl.ds(k % 2 * HB, HB), pl.ds(k // 2 * 2 * BW, 2 * BW)

    def final_dst(mb, k):
        return (od_hbm, ou_hbm)[mb].at[sum_area(k)]

    def final_remote(mb, k):
        return pltpu.make_async_remote_copy(
            src_ref=U.at[(mb,) + sum_area(k)], dst_ref=final_dst(mb, k),
            send_sem=f_send.at[mb, k], recv_sem=f_recv.at[mb, k],
            device_id=((down_s, up_s)[mb], t), device_id_type=MESH,
        )

    def goes(mb):
        return odd if mb == 0 else jnp.logical_not(up_self)

    def relay_step(mb, k):
        rows_k, cols_k = sum_area(k)
        for q in range(NT):
            blk = pl.ds((k // 2 * 2 + q % 2) * BW, BW)
            landed = RB.at[mb, q // 2, rows_k, blk]
            pltpu.make_async_copy(landed, landed, o_recv.at[mb, q, k]).wait()
        total = RB[mb, 0, rows_k, cols_k].astype(f32) + RB[mb, 1, rows_k, cols_k].astype(f32)
        first = (flip, s)[mb] == 0
        U[(mb,) + sum_area(k)] = jnp.where(first, 0.0, total).astype(bf16)

        @pl.when(goes(mb))
        def _():
            final_remote(mb, k).start()

        @pl.when(jnp.logical_not(goes(mb)))
        def _():
            pltpu.make_async_copy(U.at[(mb,) + sum_area(k)], final_dst(mb, k), f_recv.at[mb, k]).start()

    relay_copy(0).wait_recv()
    forward(0)
    RS[1] = inverse_rms(U.at[0])
    for q in range(NT):
        r_copy(1, q, (flip, q)).start()
    r_wait(0)
    gather_wait(0, 0)
    w_copy.wait()
    values(0)
    relay_copy(1).wait_recv()
    forward_sent(0)
    forward(1)
    gather_wait(0, 1)
    grads(0)
    convolve(0)
    back(0)
    finish(0)
    out_start(0, 0)
    v_copy(0).wait_send()
    r_wait(1)
    gather_wait(1, 0)
    values(1)
    gather_wait(1, 1)
    for k in range(1, CHUNKS):
        out_start(0, k)
    forward_sent(1)
    grads(1)
    convolve(1)
    back(1)
    relay_step(0, 0)
    finish(1)
    out_start(1, 0)
    out_start(1, 1)
    relay_step(0, 1)
    tap_pairs(0)
    relay_step(0, 2)
    tap_pairs(1)
    tap_sums()

    def fg_copy(q):
        return pltpu.make_async_remote_copy(
            src_ref=FG, dst_ref=fg_hbm.at[t], send_sem=fg_send.at[q], recv_sem=fg_recv.at[t],
            device_id=(s, q), device_id_type=MESH,
        )

    for q in range(NT):
        @pl.when(t != q)
        def _():
            fg_copy(q).start()

        @pl.when(t == q)
        def _():
            pltpu.make_async_copy(FG, fg_hbm.at[q], fg_recv.at[q]).start()

    DN = min(512, BW)
    tiles = D // DN

    def dw_copy(j, slot):
        return pltpu.make_async_copy(DW.at[slot], dw_hbm.at[:, cols(j, DN)], dw_sem.at[slot])

    def dw_tile(j, carry):
        slot = lax.rem(j, 2)

        @pl.when(j >= 2)
        def _():
            dw_copy(j - 2, slot).wait()

        DW[slot] = matmul(NBT[...], GV[:, cols(j, DN)]).astype(bf16)
        dw_copy(j, slot).start()
        return carry

    for k in range(CHUNKS):
        lax.fori_loop(k * tiles // CHUNKS, (k + 1) * tiles // CHUNKS, dw_tile, 0)
        if k == 0:
            relay_step(0, 3)
        if k + 2 < CHUNKS:
            out_sent(1, k)
            out_start(1, k + 2)
        relay_step(1, k)
    for j in (tiles - 2, tiles - 1):
        dw_copy(j, j % 2).wait()

    relay_copy(1).wait_send()
    for q in range(NT):
        r_copy(1, q, (flip, q)).wait_send()

        @pl.when(t != q)
        def _():
            for arr, (src, dst) in enumerate(((xd_hbm, X), (cd_hbm, C))):
                for i in range(2):
                    piece(src, dst, 0, arr, q, i, (s, q), t).wait_send()
            r_copy(0, q, (s, q)).wait_send()
            fg_copy(q).wait_send()

        pltpu.make_async_copy(FG, fg_hbm.at[q], fg_recv.at[q]).wait()
    for k in range(CHUNKS):
        out_sent(0, k)
        if k >= CHUNKS - 2:
            out_sent(1, k)
    v_copy(1).wait_send()
    for mb in range(2):
        pm_copy(mb).wait_send()
        for i in range(2):
            gv_copy(mb, i).wait_send()
    for mb in range(2):
        for k in range(CHUNKS):
            @pl.when(goes(mb))
            def _():
                final_remote(mb, k).wait_send()

            pltpu.make_async_copy(final_dst(mb, k), final_dst(mb, k), f_recv.at[mb, k]).wait()


PARTS = 16


def settle(dw_in, od_in, ou_in, dw_out, od_out, ou_out, dw_buf, od_buf, ou_buf, load_sems, save_sems):
    rows = dw_in.shape[0] // PARTS
    pieces = [(dw_in.at[pl.ds(p * rows, rows)], dw_buf.at[pl.ds(p * rows, rows)], dw_out.at[pl.ds(p * rows, rows)]) for p in range(PARTS)]
    pieces += [(od_in, od_buf, od_out), (ou_in, ou_buf, ou_out)]
    loads = [pltpu.make_async_copy(src, buf, load_sems.at[p]) for p, (src, buf, _) in enumerate(pieces)]
    saves = [pltpu.make_async_copy(buf, dst, save_sems.at[p]) for p, (_, buf, dst) in enumerate(pieces)]
    for load in loads:
        load.start()
    for load, save in zip(loads, saves):
        load.wait()
        save.start()
    for save in saves:
        save.wait()


def per_device(sections, weights, filters, down_input, down_cot, up_input, up_cot):
    w = weights[0]
    taps = filters[0]
    BW, D = w.shape
    TB = down_input.shape[1]
    CW = 2 * BW
    TOK = NT * TB
    groups, K = taps.shape
    n_groups = groups // 2
    hbm = pl.BlockSpec(memory_space=pl.ANY)
    dma = pltpu.SemaphoreType.DMA
    DN = min(512, BW)
    dw, fg, od, ou = pl.pallas_call(
        functools.partial(kernel, sections),
        out_shape=(
            jax.ShapeDtypeStruct((BW, D), bf16),
            jax.ShapeDtypeStruct((NT, n_groups, K), f32),
            jax.ShapeDtypeStruct((TB, D), bf16),
            jax.ShapeDtypeStruct((TB, D), bf16),
        ),
        in_specs=[hbm, pl.BlockSpec(memory_space=pltpu.VMEM), hbm, hbm, hbm, hbm],
        out_specs=(hbm, hbm, hbm, hbm),
        scratch_shapes=[
            pltpu.VMEM((BW, D), bf16),
            pltpu.VMEM((2, TOK, CW), bf16),
            pltpu.VMEM((2, TOK, CW), bf16),
            pltpu.VMEM((2, TOK, 128), f32),
            pltpu.VMEM((TB, D), bf16),
            pltpu.VMEM((2, TB, D), bf16),
            pltpu.VMEM((2, TB, 128), f32),
            pltpu.VMEM((n_groups, TB, 2 * TB), bf16),
            pltpu.VMEM((n_groups, TB, 2 * TB), bf16),
            pltpu.VMEM((BW, 2 * TOK), bf16),
            pltpu.VMEM((2 * TOK, D), bf16),
            pltpu.VMEM((TOK, CW), bf16),
            pltpu.VMEM((TOK, CW), bf16),
            pltpu.VMEM((2, TOK, CW), bf16),
            pltpu.VMEM((TOK, CW), bf16),
            pltpu.VMEM((2, 2, TOK, 128), f32),
            pltpu.VMEM((2, TOK, CW), bf16),
            pltpu.VMEM((2, 2, TB, D), bf16),
            pltpu.VMEM((n_groups, TB, 2 * TB), f32),
            pltpu.VMEM((n_groups, K), f32),
            pltpu.VMEM((2, BW, DN), bf16),
            dma((2, 2, NT, 2)), dma((2, 2, NT, 2)), dma((2, NT)), dma((2, NT)),
            dma((2,)), dma((2,)), dma((2,)), dma((2,)),
            dma((2, 2)), dma((2, 2)), dma((2,)), dma((2,)),
            dma((2, NT, 4)), dma((2, NT, 4)), dma((2, 4)), dma((2, 4)), dma((NT,)), dma((NT,)),
            dma, dma, dma((2,)),
        ],
        compiler_params=pltpu.CompilerParams(
            collective_id=0, has_side_effects=True, vmem_limit_bytes=60 * 1024 * 1024
        ),
        name="relay_backward",
    )(w, taps, down_input[0], down_cot[0], up_input[0], up_cot[0])
    dw, od, ou = pl.pallas_call(
        settle,
        out_shape=tuple(jax.ShapeDtypeStruct(x.shape, bf16) for x in (dw, od, ou)),
        in_specs=[hbm, hbm, hbm],
        out_specs=(hbm, hbm, hbm),
        scratch_shapes=[pltpu.VMEM(x.shape, bf16) for x in (dw, od, ou)] + [dma((PARTS + 2,)), dma((PARTS + 2,))],
        compiler_params=pltpu.CompilerParams(vmem_limit_bytes=60 * 1024 * 1024),
        name="settle",
    )(dw, od, ou)
    fg = fg.reshape(2, 2, 2, groups // NT, K)
    fg = jnp.transpose(fg[0] + fg[1], (1, 0, 2, 3)).reshape(groups, K)
    return dw[None], fg[None], od[None], ou[None]


def solution(mesh):
    row = P("section", "tensor", None)
    whole = P("section", None, None)
    return jax.shard_map(
        functools.partial(per_device, mesh.shape["section"]),
        mesh=mesh,
        in_specs=(row, whole, row, row, row, row),
        out_specs=(row, whole, row, row),
        check_vma=False,
    )
```

```python
import functools

import jax
import jax.numpy as jnp
from jax import lax
from jax.experimental import pallas as pl
from jax.experimental.pallas import tpu as pltpu
from jax.sharding import PartitionSpec as P

epsilon = 1e-06
MESH = pl.DeviceIdType.MESH
bf16 = jnp.bfloat16
f32 = jnp.float32
NT = 4


def contract_last(a, b):
    return lax.dot_general(a, b, (((1,), (1,)), ((), ())), preferred_element_type=f32)


def matmul(a, b):
    return jnp.dot(a, b, preferred_element_type=f32)


def kernel(
    sections,
    w_hbm, f_ref, xd_hbm, cd_hbm, xu_hbm, cu_hbm,
    dw_hbm, fg_hbm, od_hbm, ou_hbm,
    W, X, C, R, OWN, U, RS, T, TC, NBT, GV, VS, V, VR, G, PM, OS, RB, PAIRS, FG, DW,
    g_send, g_recv, r_send, r_recv, u_send, u_recv, v_send, v_recv,
    gv_send, gv_recv, pm_send, pm_recv, o_send, o_recv, f_send, f_recv, fg_send, fg_recv,
    w_sem, own_sem, dw_sem,
):
    S = sections
    s = lax.axis_index("section")
    t = lax.axis_index("tensor")
    h = t // 2
    c = t % 2
    sib = (s, h * 2 + (1 - c))
    TB, D = xd_hbm.shape
    BW = D // NT
    CW = 2 * BW
    TOK = NT * TB
    groups = f_ref.shape[0]
    per_block = groups // NT
    n_groups = 2 * per_block
    gw = D // groups
    flip = s + 1 - 2 * (s % 2)
    mirror = S - 1 - s
    relay = mirror + 1 - 2 * (mirror % 2)
    odd = s % 2 == 1
    down_s = lax.rem(s + S - 2, S)
    up_s = lax.rem(S - s, S)
    up_self = up_s == s

    barrier = pltpu.get_barrier_semaphore()

    def greet(dev):
        pl.semaphore_signal(barrier, inc=1, device_id=dev, device_id_type=MESH)

    for q in range(1, NT):
        greet((s, lax.rem(t + q, NT)))
    greet((relay, t))
    for q in range(NT):
        greet((flip, q))

    @pl.when(odd)
    def _():
        greet((lax.rem(s + 2, S), t))

    @pl.when(jnp.logical_not(up_self))
    def _():
        greet((up_s, t))

    w_copy = pltpu.make_async_copy(w_hbm, W, w_sem)
    w_copy.start()
    own_copy = pltpu.make_async_copy(xd_hbm, OWN, own_sem)
    own_copy.start()
    pl.semaphore_wait(barrier, 8 + jnp.where(odd, 1, 0) + jnp.where(up_self, 0, 1))

    my_rows = pl.ds(pl.multiple_of(t * TB, TB), TB)

    def piece(src, dst_ref, mb, arr, q, i, dev, src_t):
        return pltpu.make_async_remote_copy(
            src_ref=src.at[:, pl.ds((2 * i + q % 2) * BW, BW)],
            dst_ref=dst_ref.at[mb, pl.ds(pl.multiple_of(src_t * TB, TB), TB), pl.ds(i * BW, BW)],
            send_sem=g_send.at[mb, arr, q, i],
            recv_sem=g_recv.at[mb, arr, src_t, i],
            device_id=dev,
            device_id_type=MESH,
        )

    def local_piece(src, dst_ref, mb, arr, q, i):
        return pltpu.make_async_copy(
            src.at[:, pl.ds((2 * i + q % 2) * BW, BW)],
            dst_ref.at[mb, pl.ds(q * TB, TB), pl.ds(i * BW, BW)],
            g_recv.at[mb, arr, q, i],
        )

    def gather_start(arr):
        src, dst = ((xd_hbm, X), (cd_hbm, C))[arr]
        for q in range(NT):
            @pl.when(t != q)
            def _():
                for i in range(2):
                    piece(src, dst, 0, arr, q, i, (s, q), t).start()

            @pl.when(t == q)
            def _():
                for i in range(2):
                    local_piece(src, dst, 0, arr, q, i).start()

    def relay_copy(arr):
        return pltpu.make_async_remote_copy(
            src_ref=(xu_hbm, cu_hbm)[arr], dst_ref=U.at[arr],
            send_sem=u_send.at[arr], recv_sem=u_recv.at[arr],
            device_id=(relay, t), device_id_type=MESH,
        )

    relay_copy(0).start()
    gather_start(0)
    gather_start(1)

    def inverse_rms(ref):
        def step(j, acc):
            x = ref[:, pl.ds(pl.multiple_of(j * gw, gw), gw)].astype(f32)
            return acc + x * x
        acc = lax.fori_loop(0, D // gw, step, jnp.zeros((TB, gw), f32))
        mean = jnp.sum(acc, axis=1, keepdims=True) / D
        return jnp.broadcast_to(lax.rsqrt(mean + epsilon), (TB, 128))

    def r_copy(mb, q, dev):
        return pltpu.make_async_remote_copy(
            src_ref=RS.at[mb], dst_ref=R.at[mb, my_rows, :],
            send_sem=r_send.at[mb, q], recv_sem=r_recv.at[mb, t],
            device_id=dev, device_id_type=MESH,
        )

    own_copy.wait()
    RS[0] = inverse_rms(OWN)
    for q in range(NT):
        @pl.when(t != q)
        def _():
            r_copy(0, q, (s, q)).start()

        @pl.when(t == q)
        def _():
            R[0, q * TB : (q + 1) * TB, :] = RS[0]

    rows = lax.broadcasted_iota(jnp.int32, (TB, 2 * TB), 0)

    def build(gi, carry):
        g = (gi // per_block * 2 + c) * per_block + lax.rem(gi, per_block)
        taps = jnp.broadcast_to(f_ref[pl.ds(g, 1), :], (TB, TB))
        x = jnp.concatenate([taps, jnp.zeros((TB, TB), f32)], axis=1)
        step = 1
        while step < TB:
            x = jnp.where((rows & step) != 0, pltpu.roll(x, step, 1), x)
            step *= 2
        T[gi] = x.astype(bf16)
        TC[gi] = jnp.concatenate([x[:, TB:].T, x[:, :TB].T], axis=1).astype(bf16)
        return carry

    lax.fori_loop(0, n_groups, build, 0)
    relay_copy(0).wait_send()
    relay_copy(1).start()

    def gather_wait(mb, arr):
        dst = (X, C)[arr]
        for q in range(NT):
            for i in range(2):
                landed = dst.at[mb, pl.ds(q * TB, TB), pl.ds(i * BW, BW)]
                pltpu.make_async_copy(landed, landed, g_recv.at[mb, arr, q, i]).wait()

    def r_wait(mb):
        for q in range(NT):
            def wait_r():
                pltpu.make_async_copy(RS.at[mb], R.at[mb, pl.ds(q * TB, TB), :], r_recv.at[mb, q]).wait()
            if mb == 0:
                pl.when(t != q)(wait_r)
            else:
                wait_r()

    def forward(arr):
        for q in range(NT):
            for i in range(2):
                piece(U.at[arr], (X, C)[arr], 1, arr, q, i, (flip, q), t).start()

    def forward_sent(arr):
        for q in range(NT):
            for i in range(2):
                piece(U.at[arr], (X, C)[arr], 1, arr, q, i, (flip, q), t).wait_send()

    def cols(j, width=gw):
        return pl.ds(pl.multiple_of(j * width, width), width)

    def natural(gi):
        return (gi // per_block * 2 + c) * per_block + lax.rem(gi, per_block)

    def windows(x):
        return jnp.concatenate([x[i * TB : (i + 2) * TB] for i in range(NT)], axis=1)

    zero_block = jnp.zeros((TB, gw), bf16)

    def gv_copy(mb, i):
        blk = pl.ds(pl.multiple_of((2 * i + c) * BW, BW), BW)
        return pltpu.make_async_remote_copy(
            src_ref=GV.at[pl.ds(mb * TOK, TOK), blk], dst_ref=GV.at[pl.ds(mb * TOK, TOK), blk],
            send_sem=gv_send.at[mb, i], recv_sem=gv_recv.at[mb, i],
            device_id=sib, device_id_type=MESH,
        )

    def v_copy(mb):
        return pltpu.make_async_remote_copy(
            src_ref=VS, dst_ref=VR.at[mb],
            send_sem=v_send.at[mb], recv_sem=v_recv.at[mb],
            device_id=sib, device_id_type=MESH,
        )

    def pm_copy(mb):
        return pltpu.make_async_remote_copy(
            src_ref=PM.at[mb, 0], dst_ref=PM.at[mb, 1],
            send_sem=pm_send.at[mb], recv_sem=pm_recv.at[mb],
            device_id=sib, device_id_type=MESH,
        )

    VN = min(512, BW)
    RN = min(256, BW)
    UN = 2
    wide = min(512, BW)
    own_cols = pl.ds(pl.multiple_of(h * BW, BW), BW)

    def blocks(x):
        return [x[i * TB : (i + 1) * TB] for i in range(NT)]

    def values(mb):
        def norm(gi, carry):
            at = cols(gi, 2 * gw)
            scale = jnp.concatenate([R[mb], R[mb]], axis=1)
            X[mb, :, at] = (X[mb, :, at].astype(f32) * scale).astype(bf16)
            return carry

        lax.fori_loop(0, n_groups // 2, norm, 0)

        def sib_values(j, carry):
            src = (j // (BW // VN) * 2 + (1 - c)) * (BW // VN) + lax.rem(j, BW // VN)
            VS[:, cols(j, VN)] = matmul(X[mb, :, own_cols], W[:, cols(src, VN)]).astype(bf16)
            return carry

        def own_values(j, carry):
            src = (j // (BW // VN) * 2 + c) * (BW // VN) + lax.rem(j, BW // VN)
            V[:, cols(j, VN)] = matmul(X[mb, :, own_cols], W[:, cols(src, VN)]).astype(bf16)
            return carry

        lax.fori_loop(0, CW // VN, sib_values, 0)
        v_copy(mb).start()
        lax.fori_loop(0, CW // VN, own_values, 0)

        def turn(j, carry):
            n = X[mb, :, cols(h * per_block + j)].astype(f32)
            NBT[cols(j), mb * TOK : (mb + 1) * TOK] = n.T.astype(bf16)
            return carry

        lax.fori_loop(0, per_block, turn, 0)

    def mixed_grad(mb, gi):
        gm = C[mb, :, cols(gi)].astype(f32) * X[mb, :, cols(gi)].astype(f32)
        return windows(jnp.concatenate([gm.astype(bf16), zero_block], axis=0))

    def grads(mb):
        def grad(j, carry):
            gs = [j * UN + u for u in range(UN)]
            ws = [mixed_grad(mb, gi) for gi in gs]
            gvs = [matmul(T[gi], w).astype(bf16) for gi, w in zip(gs, ws)]
            for gi, gv in zip(gs, gvs):
                for i in range(NT):
                    GV[mb * TOK + i * TB : mb * TOK + (i + 1) * TB, cols(natural(gi))] = gv[:, i * gw : (i + 1) * gw]
            return carry

        lax.fori_loop(0, n_groups // UN, grad, 0)
        for i in range(2):
            gv_copy(mb, i).start()

    def convolve(mb):
        v_copy(mb).wait_recv()

        def mix(j, carry):
            gs = [j * UN + u for u in range(UN)]
            vs = [(V[:, cols(gi)].astype(f32) + VR[mb, :, cols(gi)].astype(f32)).astype(bf16) for gi in gs]
            cots = [C[mb, :, cols(gi)].astype(f32) for gi in gs]
            convs = [matmul(TC[gi], windows(jnp.concatenate([zero_block, v], axis=0))) for gi, v in zip(gs, vs)]
            for gi, v, cot, conv in zip(gs, vs, cots, convs):
                VR[mb, :, cols(gi)] = v
                conv = jnp.concatenate([conv[:, i * gw : (i + 1) * gw] for i in range(NT)], axis=0)
                G[:, cols(gi)] = (cot * conv).astype(bf16)
            return carry

        lax.fori_loop(0, n_groups // UN, mix, 0)

    def back(mb):
        for i in range(2):
            blk = pl.ds(pl.multiple_of((2 * i + 1 - c) * BW, BW), BW)
            landed = GV.at[pl.ds(mb * TOK, TOK), blk]
            pltpu.make_async_copy(landed, landed, gv_recv.at[mb, i]).wait()

        def returned(j, carry):
            res = contract_last(GV[mb * TOK : (mb + 1) * TOK, :], W[pl.ds(pl.multiple_of(j * RN, RN), RN), :])
            at = cols(h * (BW // RN) + j, RN)
            G[:, at] = (G[:, at].astype(f32) + res).astype(bf16)
            return carry

        lax.fori_loop(0, BW // RN, returned, 0)

    def finish(mb):
        def moment(j, acc):
            at = cols(j, wide)
            x = G[:, at].astype(f32) * X[mb, :, at].astype(f32)
            return acc + sum(x[:, i * gw : (i + 1) * gw] for i in range(wide // gw))

        PM[mb, 0] = lax.fori_loop(0, CW // wide, moment, jnp.zeros((TOK, gw), f32))
        pm_copy(mb).start()
        pm_copy(mb).wait_recv()
        mean = jnp.sum(PM[mb, 0] + PM[mb, 1], axis=1, keepdims=True) / D
        PM[mb, 1] = jnp.broadcast_to(mean, (TOK, gw))
        keep = jnp.where(h == 0, 1.0, 0.0).astype(f32)

        def final(j, carry):
            at = cols(j, 2 * gw)
            scale = jnp.concatenate([R[mb], R[mb]], axis=1)
            pm = jnp.concatenate([PM[mb, 1], PM[mb, 1]], axis=1)
            grad = scale * (G[:, at].astype(f32) - X[mb, :, at].astype(f32) * pm)
            OS[mb, :, at] = (grad + keep * C[mb, :, at].astype(f32)).astype(bf16)
            return carry

        lax.fori_loop(0, n_groups // 2, final, 0)

    def tap_pairs(mb):
        def pairs(j, carry):
            gs = [j * UN + u for u in range(UN)]
            ws = [mixed_grad(mb, gi) for gi in gs]
            vs = [jnp.concatenate(blocks(VR[mb, :, cols(gi)]), axis=1) for gi in gs]
            ps = [contract_last(v, w) for v, w in zip(vs, ws)]
            for gi, p in zip(gs, ps):
                PAIRS[gi] = p if mb == 0 else PAIRS[gi] + p
            return carry

        lax.fori_loop(0, n_groups // UN, pairs, 0)

    def tap_sums():
        n = TB
        while n > 8:
            half = n // 2
            for gi in range(n_groups):
                PAIRS[gi, :half] = PAIRS[gi, :half] + pltpu.roll(PAIRS[gi, half:n], 2 * TB - half, 1)
            n = half
        for gi in range(n_groups):
            x = PAIRS[gi, :8]
            for half in (4, 2, 1):
                x = x[:half] + pltpu.roll(x[half:], 2 * TB - half, 1)
            FG[gi : gi + 1, :] = x[:, :TB]

    HB = TB // 2
    CHUNKS = 4

    def out_src(mb, q, k):
        return OS.at[mb, pl.ds(q * TB + k % 2 * HB, HB), pl.ds(k // 2 * BW, BW)]

    def out_dst(mb, k):
        blk = pl.ds(pl.multiple_of((k // 2 * 2 + c) * BW, BW), BW)
        return RB.at[mb, h, pl.ds(k % 2 * HB, HB), blk]

    def out_remote(mb, q, k):
        return pltpu.make_async_remote_copy(
            src_ref=out_src(mb, q, k), dst_ref=out_dst(mb, k),
            send_sem=o_send.at[mb, q, k], recv_sem=o_recv.at[mb, t, k],
            device_id=((flip, s)[mb], q), device_id_type=MESH,
        )

    def out_start(mb, k):
        for q in range(NT):
            if mb == 0:
                out_remote(mb, q, k).start()
            else:
                @pl.when(t != q)
                def _():
                    out_remote(mb, q, k).start()

                @pl.when(t == q)
                def _():
                    pltpu.make_async_copy(out_src(mb, q, k), out_dst(mb, k), o_recv.at[mb, q, k]).start()

    def out_sent(mb, k):
        for q in range(NT):
            if mb == 0:
                out_remote(mb, q, k).wait_send()
            else:
                @pl.when(t != q)
                def _():
                    out_remote(mb, q, k).wait_send()

    def sum_area(k):
        return pl.ds(k % 2 * HB, HB), pl.ds(k // 2 * 2 * BW, 2 * BW)

    def final_dst(mb, k):
        return (od_hbm, ou_hbm)[mb].at[sum_area(k)]

    def final_remote(mb, k):
        return pltpu.make_async_remote_copy(
            src_ref=U.at[(mb,) + sum_area(k)], dst_ref=final_dst(mb, k),
            send_sem=f_send.at[mb, k], recv_sem=f_recv.at[mb, k],
            device_id=((down_s, up_s)[mb], t), device_id_type=MESH,
        )

    def goes(mb):
        return odd if mb == 0 else jnp.logical_not(up_self)

    def relay_step(mb, k):
        rows_k, cols_k = sum_area(k)
        for q in range(NT):
            blk = pl.ds((k // 2 * 2 + q % 2) * BW, BW)
            landed = RB.at[mb, q // 2, rows_k, blk]
            pltpu.make_async_copy(landed, landed, o_recv.at[mb, q, k]).wait()
        total = RB[mb, 0, rows_k, cols_k].astype(f32) + RB[mb, 1, rows_k, cols_k].astype(f32)
        first = (flip, s)[mb] == 0
        U[(mb,) + sum_area(k)] = jnp.where(first, 0.0, total).astype(bf16)

        @pl.when(goes(mb))
        def _():
            final_remote(mb, k).start()

        @pl.when(jnp.logical_not(goes(mb)))
        def _():
            pltpu.make_async_copy(U.at[(mb,) + sum_area(k)], final_dst(mb, k), f_recv.at[mb, k]).start()

    relay_copy(0).wait_recv()
    forward(0)
    RS[1] = inverse_rms(U.at[0])
    for q in range(NT):
        r_copy(1, q, (flip, q)).start()
    r_wait(0)
    gather_wait(0, 0)
    w_copy.wait()
    values(0)
    relay_copy(1).wait_recv()
    forward_sent(0)
    forward(1)
    gather_wait(0, 1)
    grads(0)
    convolve(0)
    back(0)
    finish(0)
    out_start(0, 0)
    v_copy(0).wait_send()
    r_wait(1)
    gather_wait(1, 0)
    values(1)
    gather_wait(1, 1)
    for k in range(1, CHUNKS):
        out_start(0, k)
    forward_sent(1)
    grads(1)
    convolve(1)
    back(1)
    relay_step(0, 0)
    finish(1)
    out_start(1, 0)
    out_start(1, 1)
    relay_step(0, 1)
    tap_pairs(0)
    relay_step(0, 2)
    tap_pairs(1)
    tap_sums()

    def fg_copy(q):
        return pltpu.make_async_remote_copy(
            src_ref=FG, dst_ref=fg_hbm.at[t], send_sem=fg_send.at[q], recv_sem=fg_recv.at[t],
            device_id=(s, q), device_id_type=MESH,
        )

    for q in range(NT):
        @pl.when(t != q)
        def _():
            fg_copy(q).start()

        @pl.when(t == q)
        def _():
            pltpu.make_async_copy(FG, fg_hbm.at[q], fg_recv.at[q]).start()

    DN = min(512, BW)
    tiles = D // DN

    def dw_copy(j, slot):
        return pltpu.make_async_copy(DW.at[slot], dw_hbm.at[:, cols(j, DN)], dw_sem.at[slot])

    def dw_tile(j, carry):
        slot = lax.rem(j, 2)

        @pl.when(j >= 2)
        def _():
            dw_copy(j - 2, slot).wait()

        DW[slot] = matmul(NBT[...], GV[:, cols(j, DN)]).astype(bf16)
        dw_copy(j, slot).start()
        return carry

    for k in range(CHUNKS):
        lax.fori_loop(k * tiles // CHUNKS, (k + 1) * tiles // CHUNKS, dw_tile, 0)
        if k == 0:
            relay_step(0, 3)
        if k + 2 < CHUNKS:
            out_sent(1, k)
            out_start(1, k + 2)
        relay_step(1, k)
    for j in (tiles - 2, tiles - 1):
        dw_copy(j, j % 2).wait()

    relay_copy(1).wait_send()
    for q in range(NT):
        r_copy(1, q, (flip, q)).wait_send()

        @pl.when(t != q)
        def _():
            for arr, (src, dst) in enumerate(((xd_hbm, X), (cd_hbm, C))):
                for i in range(2):
                    piece(src, dst, 0, arr, q, i, (s, q), t).wait_send()
            r_copy(0, q, (s, q)).wait_send()
            fg_copy(q).wait_send()

        pltpu.make_async_copy(FG, fg_hbm.at[q], fg_recv.at[q]).wait()
    for k in range(CHUNKS):
        out_sent(0, k)
        if k >= CHUNKS - 2:
            out_sent(1, k)
    v_copy(1).wait_send()
    for mb in range(2):
        pm_copy(mb).wait_send()
        for i in range(2):
            gv_copy(mb, i).wait_send()
    for mb in range(2):
        for k in range(CHUNKS):
            @pl.when(goes(mb))
            def _():
                final_remote(mb, k).wait_send()

            pltpu.make_async_copy(final_dst(mb, k), final_dst(mb, k), f_recv.at[mb, k]).wait()


PARTS = 4


def settle(dw_in, od_in, ou_in, dw_out, od_out, ou_out, dw_buf, od_buf, ou_buf, load_sems, save_sems):
    rows = dw_in.shape[0] // PARTS
    pieces = [(dw_in.at[pl.ds(p * rows, rows)], dw_buf.at[pl.ds(p * rows, rows)], dw_out.at[pl.ds(p * rows, rows)]) for p in range(PARTS)]
    pieces += [(od_in, od_buf, od_out), (ou_in, ou_buf, ou_out)]
    loads = [pltpu.make_async_copy(src, buf, load_sems.at[p]) for p, (src, buf, _) in enumerate(pieces)]
    saves = [pltpu.make_async_copy(buf, dst, save_sems.at[p]) for p, (_, buf, dst) in enumerate(pieces)]
    for load in loads:
        load.start()
    for load, save in zip(loads, saves):
        load.wait()
        save.start()
    for save in saves:
        save.wait()


def per_device(sections, weights, filters, down_input, down_cot, up_input, up_cot):
    w = weights[0]
    taps = filters[0]
    BW, D = w.shape
    TB = down_input.shape[1]
    CW = 2 * BW
    TOK = NT * TB
    groups, K = taps.shape
    n_groups = groups // 2
    hbm = pl.BlockSpec(memory_space=pl.ANY)
    dma = pltpu.SemaphoreType.DMA
    DN = min(512, BW)
    dw, fg, od, ou = pl.pallas_call(
        functools.partial(kernel, sections),
        out_shape=(
            jax.ShapeDtypeStruct((BW, D), bf16),
            jax.ShapeDtypeStruct((NT, n_groups, K), f32),
            jax.ShapeDtypeStruct((TB, D), bf16),
            jax.ShapeDtypeStruct((TB, D), bf16),
        ),
        in_specs=[hbm, pl.BlockSpec(memory_space=pltpu.VMEM), hbm, hbm, hbm, hbm],
        out_specs=(hbm, hbm, hbm, hbm),
        scratch_shapes=[
            pltpu.VMEM((BW, D), bf16),
            pltpu.VMEM((2, TOK, CW), bf16),
            pltpu.VMEM((2, TOK, CW), bf16),
            pltpu.VMEM((2, TOK, 128), f32),
            pltpu.VMEM((TB, D), bf16),
            pltpu.VMEM((2, TB, D), bf16),
            pltpu.VMEM((2, TB, 128), f32),
            pltpu.VMEM((n_groups, TB, 2 * TB), bf16),
            pltpu.VMEM((n_groups, TB, 2 * TB), bf16),
            pltpu.VMEM((BW, 2 * TOK), bf16),
            pltpu.VMEM((2 * TOK, D), bf16),
            pltpu.VMEM((TOK, CW), bf16),
            pltpu.VMEM((TOK, CW), bf16),
            pltpu.VMEM((2, TOK, CW), bf16),
            pltpu.VMEM((TOK, CW), bf16),
            pltpu.VMEM((2, 2, TOK, 128), f32),
            pltpu.VMEM((2, TOK, CW), bf16),
            pltpu.VMEM((2, 2, TB, D), bf16),
            pltpu.VMEM((n_groups, TB, 2 * TB), f32),
            pltpu.VMEM((n_groups, K), f32),
            pltpu.VMEM((2, BW, DN), bf16),
            dma((2, 2, NT, 2)), dma((2, 2, NT, 2)), dma((2, NT)), dma((2, NT)),
            dma((2,)), dma((2,)), dma((2,)), dma((2,)),
            dma((2, 2)), dma((2, 2)), dma((2,)), dma((2,)),
            dma((2, NT, 4)), dma((2, NT, 4)), dma((2, 4)), dma((2, 4)), dma((NT,)), dma((NT,)),
            dma, dma, dma((2,)),
        ],
        compiler_params=pltpu.CompilerParams(
            collective_id=0, has_side_effects=True, vmem_limit_bytes=60 * 1024 * 1024
        ),
        name="relay_backward",
    )(w, taps, down_input[0], down_cot[0], up_input[0], up_cot[0])
    dw, od, ou = pl.pallas_call(
        settle,
        out_shape=tuple(jax.ShapeDtypeStruct(x.shape, bf16) for x in (dw, od, ou)),
        in_specs=[hbm, hbm, hbm],
        out_specs=(hbm, hbm, hbm),
        scratch_shapes=[pltpu.VMEM(x.shape, bf16) for x in (dw, od, ou)] + [dma((PARTS + 2,)), dma((PARTS + 2,))],
        compiler_params=pltpu.CompilerParams(vmem_limit_bytes=60 * 1024 * 1024),
        name="settle",
    )(dw, od, ou)
    fg = fg.reshape(2, 2, 2, groups // NT, K)
    fg = jnp.transpose(fg[0] + fg[1], (1, 0, 2, 3)).reshape(groups, K)
    return dw[None], fg[None], od[None], ou[None]


def solution(mesh):
    row = P("section", "tensor", None)
    whole = P("section", None, None)
    return jax.shard_map(
        functools.partial(per_device, mesh.shape["section"]),
        mesh=mesh,
        in_specs=(row, whole, row, row, row, row),
        out_specs=(row, whole, row, row),
        check_vma=False,
    )
```
